32 devices in a mesh: dp: 4 (over y, core), ctx: 2 (over x), mp: 4 (over z).
Axes of the slice: x: 2, y: 2, z: 4, core: 2. Of those that a mesh axis runs over, the one named last changes fastest.
Arguments:
- block_input: bfloat16 [4, 1024, 2048], P('dp', 'ctx'), may hold values from -40 to 40
- norm_one_gain: bfloat16 [2048], P(('dp', 'ctx')), may hold values from 0.5 to 1.5
- query_weight: bfloat16 [2048, 3072], P(('dp', 'ctx'), 'mp'), may hold values from -0.125 to 0.125
- latent_weight: bfloat16 [2048, 576], P(('dp', 'ctx')), may hold values from -0.125 to 0.125
- latent_gain: bfloat16 [512], P(('dp', 'ctx')), may hold values from 0.5 to 1.5
- expand_weight: bfloat16 [512, 4096], P(('dp', 'ctx'), 'mp'), may hold values from -0.25 to 0.25
- output_weight: bfloat16 [2048, 2048], P('mp', ('dp', 'ctx')), may hold values from -0.5 to 0.5
- norm_two_gain: bfloat16 [2048], P(('dp', 'ctx')), may hold values from 0.5 to 1.5
- router_weight: bfloat16 [2048, 8], P(('dp', 'ctx')), may hold values from -0.25 to 0.25
- expert_gate: bfloat16 [8, 2048, 1408], P('mp', ('dp', 'ctx')), may hold values from -0.125 to 0.125
- expert_up: bfloat16 [8, 2048, 1408], P('mp', ('dp', 'ctx')), may hold values from -0.125 to 0.125
- expert_down: bfloat16 [8, 1408, 2048], P('mp', None, ('dp', 'ctx')), may hold values from -0.15625 to 0.15625
- shared_gate: bfloat16 [2048, 2816], P(('dp', 'ctx'), 'mp'), may hold values from -0.125 to 0.125
- shared_up: bfloat16 [2048, 2816], P(('dp', 'ctx'), 'mp'), may hold values from -0.125 to 0.125
- shared_down: bfloat16 [2816, 2048], P('mp', ('dp', 'ctx')), may hold values from -0.109375 to 0.109375
- routes: int32 [4, 1024, 6], P('dp', 'ctx'), may hold values from 0 to 7, as said below
- route_slots: int32 [4, 1024, 6], P('dp', 'ctx'), may hold values from 0 to 511, as said below
- cotangent: bfloat16 [4, 1024, 2048], P('dp', 'ctx'), may hold values from -6 to 6
Outputs:
- block_output: bfloat16 [4, 1024, 2048], P('dp', 'ctx')
- input_grad: bfloat16 [4, 1024, 2048], P('dp', 'ctx')
- norm_one_gain_grad: float32 [2048], P(('dp', 'ctx'))
- query_weight_grad: float32 [2048, 3072], P(('dp', 'ctx'), 'mp')
- latent_weight_grad: float32 [2048, 576], P(('dp', 'ctx'))
- latent_gain_grad: float32 [512], P(('dp', 'ctx'))
- expand_weight_grad: float32 [512, 4096], P(('dp', 'ctx'), 'mp')
- output_weight_grad: float32 [2048, 2048], P('mp', ('dp', 'ctx'))
- norm_two_gain_grad: float32 [2048], P(('dp', 'ctx'))
- router_weight_grad: float32 [2048, 8], P(('dp', 'ctx'))
- expert_gate_grad: float32 [8, 2048, 1408], P('mp', ('dp', 'ctx'))
- expert_up_grad: float32 [8, 2048, 1408], P('mp', ('dp', 'ctx'))
- expert_down_grad: float32 [8, 1408, 2048], P('mp', None, ('dp', 'ctx'))
- shared_gate_grad: float32 [2048, 2816], P(('dp', 'ctx'), 'mp')
- shared_up_grad: float32 [2048, 2816], P(('dp', 'ctx'), 'mp')
- shared_down_grad: float32 [2816, 2048], P('mp', ('dp', 'ctx'))
The draws below stay inside these ranges and needn't reach their ends.
Inputs may be any that keep to these rules, and one draw needn't show every extreme that they name: `routes`: each token names 6 different experts. Among the tokens of one group (one index of dp and of ctx) some expert is named by every token. `route_slots`: among the tokens of one group (one index of dp and of ctx), each pair of expert and slot is named at most once.
All inputs are finite; a program needn't handle non-finite values.
Results may differ from the reference program's by a relative error of at most 0.025.
Values may be sent and summed in bfloat16 or wider, within the bound.
No kernel may reach another device: no remote copies, remote signals or barrier semaphores. Data moves between devices by JAX's collectives and lax.ppermute only.
A program may use at most 208 MiB of HBM per device.

```python
import jax
import jax.numpy as jnp
from jax import lax

D = 2048
H = 16
QN = 128
QR = 64
VD = 128
KVR = 512
FF = 1408
TOP = 6
SEQ = 1024
TOK_DEV = 512
E = 8
SHARED = 2816
SPAN = 512
SEQS_DEV = 1
NSEQ = 4
CAP = 512
N_DP = 4
N_CTX = 2


def route_draw(key):
    blocks = N_DP * N_CTX
    key_full, key_base, key_bias, key_order, key_perm = jax.random.split(jax.random.fold_in(key, 7), 5)
    full_expert = jax.random.randint(key_full, (blocks, 1, 1), 0, E)
    base_score = jax.random.randint(key_base, (blocks, TOK_DEV, E), 0, 1024)
    bias_score = jax.random.randint(key_bias, (1, 1, E), 0, 768)
    expert_ids = jnp.arange(E, dtype=jnp.int32)
    scores = (base_score + bias_score) * E + expert_ids
    scores = jnp.where(expert_ids == full_expert, 2 ** 30, scores)
    top_scores, chosen = lax.top_k(scores, TOP)
    order_keys = jax.random.randint(key_order, (blocks, TOK_DEV, TOP), 0, 2 ** 16) * TOP + jnp.arange(TOP, dtype=jnp.int32)
    order_perm = jnp.argsort(order_keys, axis=-1)
    chosen = jnp.take_along_axis(chosen, order_perm, axis=-1).astype(jnp.int32)
    member = jnp.sum((chosen[..., None] == expert_ids).astype(jnp.int32), axis=2)
    rank_all = jnp.cumsum(member, axis=1) - member
    perm_keys = jax.random.randint(key_perm, (blocks, E, CAP), 0, 2 ** 16) * CAP + jnp.arange(CAP, dtype=jnp.int32)
    slot_perm = jnp.argsort(perm_keys, axis=-1).astype(jnp.int32).reshape(blocks, E * CAP)
    rank_chosen = jnp.take_along_axis(rank_all, chosen, axis=2)
    flat_index = (chosen * CAP + rank_chosen).reshape(blocks, TOK_DEV * TOP)
    slot_values = jnp.take_along_axis(slot_perm, flat_index, axis=1).reshape(blocks, TOK_DEV, TOP)

    def layout(values):
        shaped = values.reshape(N_DP, N_CTX, SEQS_DEV, SPAN, TOP).transpose(0, 2, 1, 3, 4)
        return shaped.reshape(NSEQ, SEQ, TOP).astype(jnp.int32)
    return (layout(chosen), layout(slot_values))


def draw_routes(key, part):
    return route_draw(key)[0]


def draw_route_slots(key, part):
    return route_draw(key)[1]


def draw_block_input(key, part):
    key_base, key_rows, key_cols = jax.random.split(jax.random.fold_in(key, 3), 3)
    row_scale = jnp.exp(jax.random.uniform(key_rows, (NSEQ, SEQ, 1), jnp.float32, jnp.log(0.3), jnp.log(3.0)))
    col_scale = jnp.exp(jax.random.uniform(key_cols, (1, 1, D), jnp.float32, jnp.log(0.3), jnp.log(3.0)))
    base_vals = jax.random.normal(key_base, (NSEQ, SEQ, D), jnp.float32)
    return jnp.clip(base_vals * row_scale * col_scale, -40.0, 40.0).astype(jnp.bfloat16)


def steps_of(key, shape, cuts, low, high):
    gain = 1.0
    for dim, parts in cuts:
        draws = jax.random.uniform(jax.random.fold_in(jax.random.fold_in(key, 6), dim), (parts,), jnp.float32, low / len(cuts), high / len(cuts))
        gain = gain * jnp.repeat(jnp.exp(draws), shape[dim] // parts).reshape((-1,) + (1,) * (len(shape) - 1 - dim))
    return gain


def bell_draw(key, extent, width, reach, cuts=(), kind=jnp.bfloat16):
    drawn = width * jax.random.normal(key, extent, jnp.float32)
    if cuts:
        drawn = drawn * steps_of(key, extent, cuts, -0.22, 0.18)
    return jnp.clip(drawn, -reach, reach).astype(kind)


def setup_inputs(seed: int = 0) -> dict:
    key_of = jax.random.split(jax.random.key(seed), 19)
    return {
        "block_input": draw_block_input(jax.random.fold_in(key_of[18], 71), 0),
        "norm_one_gain": jnp.clip(1.0 + 0.1 * jax.random.normal(key_of[1], (D,), jnp.float32), 0.5, 1.5).astype(jnp.bfloat16),
        "query_weight": bell_draw(key_of[2], (D, H * (QN + QR)), D ** -0.5, 0.125, ((0, 8), (1, 4))),
        "latent_weight": bell_draw(key_of[3], (D, KVR + QR), D ** -0.5, 0.125, ((0, 8),)),
        "latent_gain": jnp.clip(1.0 + 0.1 * jax.random.normal(key_of[4], (KVR,), jnp.float32), 0.5, 1.5).astype(jnp.bfloat16),
        "expand_weight": bell_draw(key_of[5], (KVR, H * (QN + VD)), KVR ** -0.5, 0.25, ((0, 8), (1, 4))),
        "output_weight": bell_draw(key_of[6], (H * VD, D), (H * VD // 16) ** -0.5, 0.5, ((0, 4), (1, 8))),
        "norm_two_gain": jnp.clip(1.0 + 0.1 * jax.random.normal(key_of[7], (D,), jnp.float32), 0.5, 1.5).astype(jnp.bfloat16),
        "router_weight": bell_draw(key_of[8], (D, E), (D // 4) ** -0.5, 0.25, ((0, 8),)),
        "expert_gate": bell_draw(key_of[9], (E, D, FF), D ** -0.5, 0.125, ((0, 4), (1, 8))),
        "expert_up": bell_draw(key_of[10], (E, D, FF), D ** -0.5, 0.125, ((0, 4), (1, 8))),
        "expert_down": bell_draw(key_of[11], (E, FF, D), FF ** -0.5, 0.15625, ((0, 4), (2, 8))),
        "shared_gate": bell_draw(key_of[12], (D, SHARED), D ** -0.5, 0.125, ((0, 8), (1, 4))),
        "shared_up": bell_draw(key_of[13], (D, SHARED), D ** -0.5, 0.125, ((0, 8), (1, 4))),
        "shared_down": bell_draw(key_of[14], (SHARED, D), SHARED ** -0.5, 0.109375, ((0, 4), (1, 8))),
        "routes": draw_routes(jax.random.fold_in(key_of[18], 71), 0),
        "route_slots": draw_route_slots(jax.random.fold_in(key_of[18], 71), 0),
        "cotangent": bell_draw(key_of[17], (NSEQ, SEQ, D), 1.0, 6.0, ((0, 4), (1, 2))),
    }


EPSILON = 1e-06
HIGHEST = lax.Precision.HIGHEST

@jax.custom_vjp
def low(v):
    return lax.optimization_barrier(v.astype(jnp.bfloat16)).astype(jnp.float32)

@jax.custom_vjp
def low_back(v):
    return v

def low_keep(v):
    return (low(v), None)

def low_pass(kept, grad):
    return (grad,)

def back_keep(v):
    return (v, None)

def back_low(kept, grad):
    return (low(grad),)
low.defvjp(low_keep, low_pass)
low_back.defvjp(back_keep, back_low)

def matmul(left_in, right_in):
    return jnp.dot(left_in, right_in, precision=HIGHEST, preferred_element_type=jnp.float32)

def rms_norm(values, gain_vec):
    return values * lax.rsqrt(lax.optimization_barrier(jnp.mean(values * values, axis=-1, keepdims=True)) + EPSILON) * gain_vec

def rotate(values, cosines, sines):
    half_dim = values.shape[-1] // 2
    first_half = values[..., :half_dim]
    second_half = values[..., half_dim:]
    return jnp.concatenate([first_half * cosines - second_half * sines, second_half * cosines + first_half * sines], axis=-1)

def to_blocks(values):
    shaped = values.reshape(N_DP, SEQS_DEV, N_CTX, SPAN, -1).transpose(0, 2, 1, 3, 4)
    return shaped.reshape(N_DP * N_CTX, TOK_DEV, -1)

def from_blocks(values):
    shaped = values.reshape(N_DP, N_CTX, SEQS_DEV, SPAN, -1).transpose(0, 2, 1, 3, 4)
    return shaped.reshape(NSEQ * SEQ, -1)

def attend(block_parts):
    query_blk, pair_blk, rope_blk = block_parts
    score_scale = (QN + QR) ** (-0.5)
    logits = jnp.einsum('qhd,khd->hqk', query_blk[..., :QN], pair_blk[..., :QN], precision=HIGHEST)
    logits = logits + jnp.einsum('qhd,kd->hqk', query_blk[..., QN:], rope_blk, precision=HIGHEST)
    logits = low_back(logits * score_scale)
    visible = jnp.arange(SEQ)[:, None] >= jnp.arange(SEQ)[None, :]
    score_exp = jnp.where(visible[None], jnp.exp(logits), 0.0)
    attn_probs = low(score_exp / lax.optimization_barrier(jnp.sum(score_exp, axis=-1, keepdims=True)))
    return jnp.einsum('hqk,khd->qhd', attn_probs, pair_blk[..., QN:], precision=HIGHEST)

def reference(block_input, norm_one_gain, query_weight, latent_weight, latent_gain, expand_weight, output_weight, norm_two_gain, router_weight, expert_gate, expert_up, expert_down, shared_gate, shared_up, shared_down, routes, route_slots, cotangent):
    route_rows = to_blocks(routes.reshape(NSEQ * SEQ, TOP))
    slot_rows = to_blocks(route_slots.reshape(NSEQ * SEQ, TOP))

    def forward(x_in, gain_one, query_in, latent_in, gain_latent, expand_in, output_in, gain_two, router_in, gate_in, up_in, down_in, sgate_in, sup_in, sdown_in):
        tokens = x_in.reshape(NSEQ * SEQ, D)
        h_one = low(rms_norm(tokens, gain_one))
        half_dim = QR // 2
        frequencies = 10000.0 ** (-jnp.arange(half_dim, dtype=jnp.float32) / half_dim)
        angles = jnp.tile(jnp.arange(SEQ, dtype=jnp.float32)[:, None] * frequencies[None, :], (NSEQ, 1))
        cosines = jnp.cos(angles)
        sines = jnp.sin(angles)
        q_raw = low_back(matmul(h_one, query_in)).reshape(-1, H, QN + QR)
        queries = low(jnp.concatenate([q_raw[..., :QN], rotate(q_raw[..., QN:], cosines[:, None, :], sines[:, None, :])], axis=-1))
        latent = low_back(matmul(h_one, latent_in))
        compressed = low(rms_norm(latent[:, :KVR], gain_latent))
        key_rope = low(rotate(latent[:, KVR:], cosines, sines))
        key_vals = low(matmul(compressed, expand_in)).reshape(-1, H, QN + VD)
        heads_out = lax.map(jax.checkpoint(attend), (queries.reshape(NSEQ, SEQ, H, QN + QR), key_vals.reshape(NSEQ, SEQ, H, QN + VD), key_rope.reshape(NSEQ, SEQ, QR)))
        heads_out = low(low_back(heads_out.reshape(NSEQ * SEQ, H * VD)))
        mixed_rows = tokens + low_back(matmul(heads_out, output_in))
        h_two = low(rms_norm(mixed_rows, gain_two))
        logits = low_back(matmul(h_two, router_in))
        router_exp = jnp.exp(logits)
        router_probs = router_exp / lax.optimization_barrier(jnp.sum(router_exp, axis=-1, keepdims=True))
        shared_gate_vals = low_back(matmul(h_two, sgate_in))
        shared_up_vals = low_back(matmul(h_two, sup_in))
        shared_act = low(jax.nn.silu(shared_gate_vals) * shared_up_vals)
        shared_out = low_back(matmul(shared_act, sdown_in))

        def experts(block_parts):
            block_rows, block_probs, block_routes, block_slots = block_parts
            slot_index = block_routes * CAP + block_slots
            token_ids = jnp.broadcast_to(jnp.arange(TOK_DEV, dtype=jnp.int32)[:, None], slot_index.shape)
            source = jnp.zeros((E * CAP,), jnp.int32).at[slot_index.reshape(-1)].set(token_ids.reshape(-1))
            filled = jnp.zeros((E * CAP,), jnp.float32).at[slot_index.reshape(-1)].set(1.0)
            dispatched = (block_rows[source] * filled[:, None]).reshape(E, CAP, D)
            gate_vals = low_back(jnp.einsum('ecd,edf->ecf', dispatched, gate_in, precision=HIGHEST))
            up_vals = low_back(jnp.einsum('ecd,edf->ecf', dispatched, up_in, precision=HIGHEST))
            expert_act = low(jax.nn.silu(gate_vals) * up_vals)
            expert_out = low(low_back(jnp.einsum('ecf,efd->ecd', expert_act, down_in, precision=HIGHEST))).reshape(E * CAP, D)
            chosen = jnp.take_along_axis(block_probs, block_routes, axis=1)
            return lax.optimization_barrier(jnp.sum(chosen[:, :, None] * expert_out[slot_index], axis=1))
        routed = from_blocks(lax.map(jax.checkpoint(experts), (to_blocks(h_two), to_blocks(router_probs), route_rows, slot_rows)))
        result = mixed_rows + shared_out + routed
        return result.reshape(NSEQ, SEQ, D)
    floats = (block_input.astype(jnp.float32), norm_one_gain.astype(jnp.float32), query_weight.astype(jnp.float32), latent_weight.astype(jnp.float32), latent_gain.astype(jnp.float32), expand_weight.astype(jnp.float32), output_weight.astype(jnp.float32), norm_two_gain.astype(jnp.float32), router_weight.astype(jnp.float32), expert_gate.astype(jnp.float32), expert_up.astype(jnp.float32), expert_down.astype(jnp.float32), shared_gate.astype(jnp.float32), shared_up.astype(jnp.float32), shared_down.astype(jnp.float32))
    block_value, pull_back = jax.vjp(forward, *floats)
    grads_all = pull_back(cotangent.astype(jnp.float32))
    return (block_value.astype(jnp.bfloat16), grads_all[0].astype(jnp.bfloat16), grads_all[1], grads_all[2], grads_all[3], grads_all[4], grads_all[5], grads_all[6], grads_all[7], grads_all[8], grads_all[9], grads_all[10], grads_all[11], grads_all[12], grads_all[13], grads_all[14])
```

```python
import jax
import jax.numpy as jnp
from jax import lax
from jax.experimental import pallas as pl
from jax.experimental.pallas import tpu as pltpu
from jax.sharding import PartitionSpec as P

D = 2048
QN = 128
QR = 64
VD = 128
KVR = 512
TOP = 6
LANES = 128
EPSILON = 1e-06
F32 = jnp.float32
BF16 = jnp.bfloat16


def dot_nn(left_in, right_in):
    return lax.dot_general(left_in, right_in, (((1,), (0,)), ((), ())), preferred_element_type=F32)


def dot_tn(left_in, right_in):
    return lax.dot_general(left_in, right_in, (((0,), (0,)), ((), ())), preferred_element_type=F32)


def dot_nt(left_in, right_in):
    return lax.dot_general(left_in, right_in, (((1,), (1,)), ((), ())), preferred_element_type=F32)


def norm_rows(values, gain_vec):
    inverse = lax.rsqrt(jnp.mean(values * values, axis=-1, keepdims=True) + EPSILON)
    normed = values * inverse
    return (normed * gain_vec, normed, inverse)


def norm_back(grad_out, normed, inverse, gain_vec):
    scaled = grad_out * gain_vec
    grad_in = inverse * (scaled - normed * jnp.mean(normed * scaled, axis=-1, keepdims=True))
    return (grad_in, jnp.sum(grad_out * normed, axis=0))


def rotate(values, cosines, sines):
    half_dim = values.shape[-1] // 2
    first_half = values[..., :half_dim]
    second_half = values[..., half_dim:]
    return jnp.concatenate(
        [first_half * cosines - second_half * sines, second_half * cosines + first_half * sines],
        axis=-1,
    )


def tie(values, *after):
    return lax.optimization_barrier((values, after))[0]


def block_copy(order, values, axis, blocks):
    rows, cols = values.shape
    if axis == 0:
        shape, index = (rows // blocks, cols), lambda i: (i, 0)
        source = lambda i, order_ref: (order_ref[i], 0)
    else:
        shape, index = (rows, cols // blocks), lambda i: (0, i)
        source = lambda i, order_ref: (0, order_ref[i])

    def body(order_ref, in_ref, out_ref):
        out_ref[...] = in_ref[...]

    return pl.pallas_call(
        body,
        out_shape=jax.ShapeDtypeStruct(values.shape, values.dtype),
        grid_spec=pltpu.PrefetchScalarGridSpec(
            num_scalar_prefetch=1,
            grid=(blocks,),
            in_specs=[pl.BlockSpec(shape, source)],
            out_specs=pl.BlockSpec(shape, lambda i, order_ref: index(i)),
        ),
        cost_estimate=pl.CostEstimate(
            flops=0, transcendentals=0, bytes_accessed=2 * values.size * values.dtype.itemsize
        ),
    )(order, values)


def pad_cols(values, width):
    return jnp.pad(values, ((0, 0), (0, width - values.shape[1])))


def up_to(count, step):
    return -(-count // step) * step


class Plan:
    def __init__(self, sizes):
        self.dp = sizes["dp"]
        self.ctx = sizes["ctx"]
        self.group = self.dp * self.ctx
        self.fast = self.dp == 4 and self.ctx == 2
        if self.fast:
            me = lax.axis_index("dp") * 2 + lax.axis_index("ctx")
            ids = jnp.arange(8, dtype=jnp.int32)
            self.order = (self.swap(ids) ^ me).astype(jnp.int32)
            self.inverse = self.swap(ids ^ me).astype(jnp.int32)

    @staticmethod
    def swap(bits):
        return (bits & 1) | (((bits >> 1) & 1) << 2) | (((bits >> 2) & 1) << 1)

    @staticmethod
    def over_core(values):
        return lax.ppermute(values, "dp", [(i, i ^ 1) for i in range(4)])

    @staticmethod
    def over_y(values):
        return lax.ppermute(values, "dp", [(i, i ^ 2) for i in range(4)])

    @staticmethod
    def over_x(values):
        return lax.ppermute(values, "ctx", [(0, 1), (1, 0)])

    def to_own(self, values, axis):
        return block_copy(self.order, values, axis, 8) if self.fast else values

    def to_natural(self, values, axis):
        return block_copy(self.inverse, values, axis, 8) if self.fast else values

    def gather(self, shard, axis, x_last):
        if not self.fast:
            full = lax.all_gather(shard, ("dp", "ctx"), axis=axis, tiled=True)
            return full, (full,)
        from_x = self.over_x(shard)
        from_y = self.over_y(shard)
        from_xy = self.over_x(from_y) if x_last else self.over_y(from_x)
        own = [shard, from_x, from_y, from_xy]
        full = jnp.concatenate(own + [self.over_core(v) for v in own], axis=axis)
        return full, (from_x, from_y)

    def reduce(self, part, size, axis, x_first):
        if not self.fast:
            whole = part(0, self.group).astype(BF16)
            return lax.psum_scatter(
                whole, ("dp", "ctx"), scatter_dimension=axis, tiled=True
            ).astype(F32)

        def cut(values, i):
            return lax.slice_in_dim(values, i * size, (i + 1) * size, axis=axis)

        sent = self.over_core(part(4, 8).astype(BF16))
        held = (part(0, 4) + sent.astype(F32)).astype(BF16)
        first, second = (1, 2) if x_first else (2, 1)
        over_first, over_second = (
            (self.over_x, self.over_y) if x_first else (self.over_y, self.over_x)
        )
        here = over_first(cut(held, first))
        there = over_first(cut(held, 3))
        passed = (cut(held, second).astype(F32) + there.astype(F32)).astype(BF16)
        last = over_second(passed)
        return cut(held, 0).astype(F32) + here.astype(F32) + last.astype(F32)


def local(
    sizes,
    block_input,
    norm_one_gain,
    query_weight,
    latent_weight,
    latent_gain,
    expand_weight,
    output_weight,
    norm_two_gain,
    router_weight,
    expert_gate,
    expert_up,
    expert_down,
    shared_gate,
    shared_up,
    shared_down,
    routes,
    route_slots,
    cotangent,
):
    plan = Plan(sizes)
    fast = plan.fast
    n_mp = sizes["mp"]
    mp_index = lax.axis_index("mp")
    seq_count, span_len = block_input.shape[0], block_input.shape[1]
    rows = seq_count * span_len
    shard_rows = rows // n_mp
    head_dim = QN + QR
    pair_dim = QN + VD
    q_cols = query_weight.shape[1]
    local_heads = q_cols // head_dim
    experts_here = expert_gate.shape[0]
    experts_all = router_weight.shape[1]
    hidden = expert_gate.shape[2]
    shared_cols = shared_gate.shape[1]
    shared_pad = up_to(shared_cols, 2 * LANES)
    block = norm_one_gain.shape[0]
    rank_block = expand_weight.shape[0]
    slots_all = experts_here * rows

    attn_in = jnp.concatenate([query_weight, latent_weight], axis=1)
    shared_in = jnp.concatenate(
        [
            pad_cols(shared_gate, shared_pad),
            pad_cols(shared_up, shared_pad),
            pad_cols(router_weight, LANES),
        ],
        axis=1,
    )
    down_shared = jnp.pad(shared_down, ((0, shared_pad - shared_cols), (0, 0)))
    if fast:
        folds = expand_weight.shape[1] // block
        gains = jnp.concatenate(
            [
                norm_one_gain[None, :],
                norm_two_gain[None, :],
                pad_cols(latent_gain[None, :], block),
                jnp.zeros((13, block), BF16),
            ],
            axis=0,
        )
        out_rows = output_weight.shape[0]
        small_in = jnp.concatenate(
            [gains, output_weight]
            + [expand_weight[:, j * block : (j + 1) * block] for j in range(folds)],
            axis=0,
        )
        small_full, small_done = plan.gather(small_in, 1, False)
        attn_full, attn_done = plan.gather(attn_in, 0, True)
        gain_one = small_full[0].astype(F32)
        gain_two = small_full[1].astype(F32)
        rank_rel = small_full[2].reshape(8, block)[:, :rank_block].astype(F32)
        place = (plan.inverse[:, None] == jnp.arange(8, dtype=jnp.int32)[None, :]).astype(F32)
        gain_latent = jnp.sum(place[:, :, None] * rank_rel[None, :, :], axis=1).reshape(KVR)
        output_full = small_full[16 : 16 + out_rows]
        expand_rel = small_full[16 + out_rows :].reshape(folds, rank_block, 8, block)
        expand_rel = expand_rel.transpose(2, 1, 0, 3).reshape(8 * rank_block, folds * block)
        expand_full = plan.to_natural(expand_rel, 0)
    else:
        gain_one = lax.all_gather(norm_one_gain, ("dp", "ctx"), tiled=True).astype(F32)
        gain_two = lax.all_gather(norm_two_gain, ("dp", "ctx"), tiled=True).astype(F32)
        gain_latent = lax.all_gather(latent_gain, ("dp", "ctx"), tiled=True).astype(F32)
        attn_full, attn_done = plan.gather(attn_in, 0, True)
        output_full, small_done = plan.gather(output_weight, 1, False)
        expand_full, _ = plan.gather(expand_weight, 0, False)
    down_shards = [expert_down[e] for e in range(experts_here)]
    down_shards, down_shared, shared_in = tie(
        (down_shards, down_shared, shared_in), *attn_done, *small_done
    )
    down_full = []
    for e in range(experts_here):
        full, _ = plan.gather(down_shards[e], 1, e % 2 == 0)
        down_full.append(full)
    sdown_full, _ = plan.gather(down_shared, 1, True)
    shared_full, shared_done = plan.gather(shared_in, 0, False)
    gate_shard, up_shard = tie((expert_gate, expert_up), *shared_done)
    gate_full, _ = plan.gather(gate_shard, 1, True)
    up_full, _ = plan.gather(up_shard, 1, False)
    query_full = attn_full[:, :q_cols]
    latent_full = attn_full[:, q_cols:]
    router_full = shared_full[:, 2 * shared_pad : 2 * shared_pad + experts_all]
    sboth_full = shared_full[:, : 2 * shared_pad]

    ctx_index = lax.axis_index("ctx")
    half_dim = QR // 2
    frequencies = 10000.0 ** (-jnp.arange(half_dim, dtype=F32) / half_dim)
    steps = jnp.arange(span_len, dtype=jnp.int32)
    query_pos = ctx_index * span_len + steps
    angles = jnp.tile(query_pos.astype(F32)[:, None] * frequencies[None, :], (seq_count, 1))
    cosines = jnp.cos(angles)
    sines = jnp.sin(angles)
    route_rows = routes.reshape(rows, TOP)
    slot_rows = route_slots.reshape(rows, TOP)
    slot_ids = jnp.arange(rows, dtype=jnp.int32)
    hits = []
    for e in range(experts_here):
        named = route_rows == mp_index * experts_here + e
        slot = jnp.sum(jnp.where(named, slot_rows + 1, 0), axis=-1) - 1
        hits.append(slot[:, None] == slot_ids[None, :])
    hit = jnp.concatenate(hits, axis=1)
    one_hot = hit.astype(BF16)

    x_low = plan.to_own(block_input.reshape(rows, D), 1)
    g_low = plan.to_own(cotangent.reshape(rows, D), 1)
    row_start = mp_index * shard_rows
    x_own = lax.dynamic_slice_in_dim(x_low, row_start, shard_rows, axis=0).astype(F32)
    g_own = lax.dynamic_slice_in_dim(g_low, row_start, shard_rows, axis=0).astype(F32)
    h_one = norm_rows(x_low.astype(F32), gain_one)[0].astype(BF16)
    attn_raw = dot_nn(h_one, attn_full)
    latent = attn_raw[:, q_cols:]
    comp_f = norm_rows(latent[:, :KVR], gain_latent)[0]
    key_rope = rotate(latent[:, KVR:], cosines, sines)
    shared_kv = jnp.concatenate([comp_f, key_rope], axis=1).astype(BF16)
    shared_kv = shared_kv.reshape(seq_count, span_len, KVR + QR)
    if plan.ctx == 2:
        other_kv = plan.over_x(shared_kv)
        kv_all = jnp.concatenate([shared_kv, other_kv], axis=1)
        key_pos = jnp.concatenate([query_pos, (1 - ctx_index) * span_len + steps])
    else:
        kv_all = lax.all_gather(shared_kv, "ctx", axis=1, tiled=True)
        key_pos = jnp.arange(plan.ctx * span_len, dtype=jnp.int32)
    seq_len = key_pos.shape[0]
    comp_all = kv_all[..., :KVR].reshape(seq_count * seq_len, KVR)
    rope_all = kv_all[..., KVR:]
    q_raw = attn_raw[:, :q_cols].reshape(rows, local_heads, head_dim)
    score_scale = head_dim ** (-0.5)
    queries = jnp.concatenate(
        [q_raw[..., :QN], rotate(q_raw[..., QN:], cosines[:, None, :], sines[:, None, :])], axis=-1
    ).astype(BF16)
    queries = queries.reshape(seq_count, span_len, local_heads, head_dim)
    pairs = dot_nn(comp_all, expand_full).astype(BF16)
    pairs = pairs.reshape(seq_count, seq_len, local_heads, pair_dim)
    keys = jnp.concatenate(
        [
            pairs[..., :QN],
            jnp.broadcast_to(rope_all[:, :, None, :], (seq_count, seq_len, local_heads, QR)),
        ],
        axis=-1,
    )
    vals = pairs[..., QN:]
    visible = query_pos[:, None] >= key_pos[None, :]
    scores = jnp.einsum("sqhd,skhd->shqk", queries, keys, preferred_element_type=F32) * score_scale
    score_exp = jnp.where(visible, jnp.exp(scores), 0.0)
    totals = jnp.sum(score_exp, axis=-1, keepdims=True)
    probs = (score_exp / totals).astype(BF16)
    heads_out = jnp.einsum("shqk,skhd->sqhd", probs, vals, preferred_element_type=F32)
    heads_flat = heads_out.reshape(rows, local_heads * VD).astype(BF16)
    attn_part = dot_nn(heads_flat, output_full).astype(BF16)
    attn_sum = lax.psum_scatter(attn_part, "mp", scatter_dimension=0, tiled=True)
    mixed = x_own + attn_sum.astype(F32)
    h_two_f, normed_two, inverse_two = norm_rows(mixed, gain_two)
    h_two = lax.all_gather(h_two_f.astype(BF16), "mp", axis=0, tiled=True)

    g_slots = dot_tn(one_hot, g_low).astype(BF16).reshape(experts_here, rows, D)
    act_back = [dot_nt(g_slots[e], down_full[e]).astype(BF16) for e in range(experts_here)]
    shared_back = dot_nt(g_low, sdown_full)

    router_exp = jnp.exp(dot_nn(h_two, router_full))
    router_probs = router_exp / jnp.sum(router_exp, axis=-1, keepdims=True)
    shared_vals = dot_nn(h_two, sboth_full)
    shared_a = shared_vals[:, :shared_pad]
    shared_b = shared_vals[:, shared_pad:]
    shared_sig = jax.nn.sigmoid(shared_a)
    shared_act = (shared_a * shared_sig * shared_b).astype(BF16)
    grad_shared_gate = shared_back * shared_b * shared_sig * (1.0 + shared_a * (1.0 - shared_sig))
    grad_shared_up = shared_back * shared_a * shared_sig
    grad_shared = jnp.concatenate([grad_shared_gate, grad_shared_up], axis=1).astype(BF16)

    probs_here = lax.dynamic_slice_in_dim(router_probs, mp_index * experts_here, experts_here, 1)
    dispatched = dot_tn(one_hot, h_two).astype(BF16).reshape(experts_here, rows, D)
    hit_parts = hit.reshape(rows, experts_here, rows)
    slot_gate = jnp.sum(jnp.where(hit_parts, probs_here[:, :, None], 0.0), axis=0)
    grad_gates, grad_ups, act_gated, slot_grads = [], [], [], []
    for e in range(experts_here):
        gate_vals = dot_nn(dispatched[e], gate_full[e])
        up_vals = dot_nn(dispatched[e], up_full[e])
        sig = jax.nn.sigmoid(gate_vals)
        act = gate_vals * sig * up_vals
        gated = slot_gate[e][:, None]
        back = act_back[e].astype(F32)
        slot_grads.append(jnp.sum(back * act, axis=-1))
        back = back * gated
        grad_gates.append((back * up_vals * sig * (1.0 + gate_vals * (1.0 - sig))).astype(BF16))
        grad_ups.append((back * gate_vals * sig).astype(BF16))
        act_gated.append((act * gated).astype(BF16))
    grad_slots = []
    for e in range(experts_here):
        grad_slot = dot_nt(grad_gates[e], gate_full[e]) + dot_nt(grad_ups[e], up_full[e])
        grad_slots.append(grad_slot.astype(BF16))
    grad_h_two = dot_nn(one_hot, jnp.concatenate(grad_slots, axis=0)) + dot_nt(
        grad_shared, sboth_full
    )
    expert_ids = jnp.arange(LANES, dtype=jnp.int32)
    grad_probs_part = jnp.zeros((rows, LANES), F32)
    for e in range(experts_here):
        of_token = jnp.sum(jnp.where(hits[e], slot_grads[e][None, :], 0.0), axis=1)
        grad_probs_part = grad_probs_part + jnp.where(
            expert_ids[None, :] == mp_index * experts_here + e, of_token[:, None], 0.0
        )
    back_part = jnp.concatenate([grad_h_two.astype(BF16), grad_probs_part.astype(BF16)], axis=1)
    back_sum = lax.psum_scatter(back_part, "mp", scatter_dimension=0, tiled=True).astype(F32)

    expert_out = [dot_nn(act_gated[e], down_full[e]).astype(BF16) for e in range(experts_here)]
    ff_part = dot_nn(one_hot, jnp.concatenate(expert_out, axis=0)) + dot_nn(shared_act, sdown_full)
    ff_sum = lax.psum_scatter(ff_part.astype(BF16), "mp", scatter_dimension=0, tiled=True)
    result_own = (mixed + ff_sum.astype(F32)).astype(BF16)
    result = plan.to_natural(lax.all_gather(result_own, "mp", axis=0, tiled=True), 1)

    def by_rows(left_in, right_in):
        return lambda a, b: dot_tn(left_in[:, a * block : b * block], right_in)

    def by_cols(left_in, right_in):
        return lambda a, b: dot_tn(left_in, right_in[:, a * block : b * block])

    down_grads = [
        plan.reduce(by_cols(act_gated[e], g_slots[e]), block, 1, e % 2 == 0)
        for e in range(experts_here)
    ]
    sdown_grad = plan.reduce(by_cols(shared_act, g_low), block, 1, True)[:shared_cols]
    sboth_grad = plan.reduce(by_rows(h_two, grad_shared), block, 0, False)
    gate_grads = [
        plan.reduce(by_rows(dispatched[e], grad_gates[e]), block, 0, e % 2 == 0)
        for e in range(experts_here)
    ]
    up_grads = [
        plan.reduce(by_rows(dispatched[e], grad_ups[e]), block, 0, e % 2 == 1)
        for e in range(experts_here)
    ]

    probs_own = lax.dynamic_slice_in_dim(router_probs, row_start, shard_rows, axis=0)
    grad_probs = back_sum[:, D : D + experts_all]
    grad_logits = (
        probs_own * (grad_probs - jnp.sum(probs_own * grad_probs, axis=-1, keepdims=True))
    ).astype(BF16)
    grad_two = back_sum[:, :D] + dot_nt(grad_logits, router_full)
    grad_norm, norm_two_part = norm_back(grad_two, normed_two, inverse_two, gain_two)
    grad_mixed = g_own + grad_norm
    mixed_part = jnp.concatenate([grad_mixed.astype(BF16), pad_cols(grad_logits, LANES)], axis=1)
    mixed_all = lax.all_gather(mixed_part, "mp", axis=0, tiled=True)
    grad_low = mixed_all[:, :D]
    grad_heads = dot_nt(grad_low, output_full).astype(BF16)
    router_part = dot_tn(mixed_all[:, D : D + experts_all], h_two)

    grad_out = grad_heads.reshape(seq_count, span_len, local_heads, VD)
    probs_f = probs.astype(F32)
    grad_probs_attn = jnp.einsum("sqhd,skhd->shqk", grad_out, vals, preferred_element_type=F32)
    row_delta = jnp.sum(probs_f * grad_probs_attn, axis=-1, keepdims=True)
    grad_scores = (probs_f * (grad_probs_attn - row_delta) * score_scale).astype(BF16)
    grad_vals = jnp.einsum("shqk,sqhd->skhd", probs, grad_out, preferred_element_type=F32)
    grad_q = jnp.einsum("shqk,skhd->sqhd", grad_scores, keys, preferred_element_type=F32)
    grad_k = jnp.einsum("shqk,sqhd->skhd", grad_scores, queries, preferred_element_type=F32)
    grad_rope = jnp.sum(grad_k[..., QN:], axis=2)
    grad_pairs = jnp.concatenate([grad_k[..., :QN], grad_vals], axis=-1).astype(BF16)
    grad_pairs = grad_pairs.reshape(seq_count * seq_len, local_heads * pair_dim)
    grad_comp = dot_nt(grad_pairs, expand_full).reshape(seq_count, seq_len, KVR)
    grad_kv = jnp.concatenate([grad_comp, grad_rope], axis=-1)
    if plan.ctx == 2:
        from_other = plan.over_x(grad_kv[:, span_len:].astype(BF16))
        grad_kv = grad_kv[:, :span_len] + from_other.astype(F32)
    else:
        grad_kv = lax.psum_scatter(grad_kv, "ctx", scatter_dimension=1, tiled=True)
    grad_kv = grad_kv.reshape(rows, KVR + QR).astype(BF16)
    grad_kv = lax.psum_scatter(grad_kv, "mp", scatter_dimension=0, tiled=True).astype(F32)
    grad_q = grad_q.reshape(rows, local_heads, head_dim)
    grad_q_raw = jnp.concatenate(
        [grad_q[..., :QN], rotate(grad_q[..., QN:], cosines[:, None, :], -sines[:, None, :])],
        axis=-1,
    )
    grad_q_raw = grad_q_raw.reshape(rows, q_cols).astype(BF16)
    query_part = dot_nt(grad_q_raw, query_full).astype(BF16)
    grad_one = lax.psum_scatter(query_part, "mp", scatter_dimension=0, tiled=True).astype(F32)
    latent_own = lax.dynamic_slice_in_dim(latent, row_start, shard_rows, axis=0)
    _, comp_normed, comp_inverse = norm_rows(latent_own[:, :KVR], gain_latent)
    grad_comp_in, latent_gain_part = norm_back(
        grad_kv[:, :KVR], comp_normed, comp_inverse, gain_latent
    )
    cos_own = lax.dynamic_slice_in_dim(cosines, row_start, shard_rows, axis=0)
    sin_own = lax.dynamic_slice_in_dim(sines, row_start, shard_rows, axis=0)
    grad_latent = jnp.concatenate(
        [grad_comp_in, rotate(grad_kv[:, KVR:], cos_own, -sin_own)], axis=1
    ).astype(BF16)
    latent_all = lax.all_gather(grad_latent, "mp", axis=0, tiled=True)
    grad_one = grad_one + dot_nt(grad_latent, latent_full)
    _, normed_one, inverse_one = norm_rows(x_own, gain_one)
    grad_tokens, norm_one_part = norm_back(grad_one, normed_one, inverse_one, gain_one)
    input_own = (grad_mixed + grad_tokens).astype(BF16)
    input_grad = plan.to_natural(lax.all_gather(input_own, "mp", axis=0, tiled=True), 1)

    output_grad = plan.reduce(by_cols(heads_flat, grad_low), block, 1, True)
    query_grad = plan.reduce(by_rows(h_one, grad_q_raw), block, 0, True)
    if fast:
        expand_whole = plan.to_own(dot_tn(comp_all, grad_pairs).astype(BF16), 0)
    else:
        expand_whole = dot_tn(comp_all, grad_pairs)
    expand_grad = plan.reduce(
        lambda a, b: expand_whole[a * rank_block : b * rank_block].astype(F32),
        rank_block,
        0,
        False,
    )
    latent_grad = plan.reduce(by_rows(h_one, latent_all), block, 0, False)

    if fast:
        to_rel = (plan.order[:, None] == jnp.arange(8, dtype=jnp.int32)[None, :]).astype(F32)
        latent_rel = jnp.sum(
            to_rel[:, :, None] * latent_gain_part.reshape(1, 8, rank_block), axis=1
        )
        router_once = jnp.where(mp_index == 0, router_part, 0.0)
        router_rel = router_once.reshape(experts_all, 8, block).transpose(1, 0, 2)
        small = jnp.concatenate(
            [
                norm_one_part.reshape(8, block),
                norm_two_part.reshape(8, block),
                router_rel.reshape(8, experts_all * block),
                pad_cols(latent_rel, LANES),
            ],
            axis=1,
        )
        small = small[:4] + plan.over_core(small[4:])
        small = small[:2] + plan.over_y(small[2:])
        small = small[:1] + plan.over_x(small[1:])
        small = lax.psum(small, "mp")[0]
        norm_one_grad = small[:block]
        norm_two_grad = small[block : 2 * block]
        router_grad = small[2 * block : (2 + experts_all) * block].reshape(experts_all, block).T
        latent_gain_grad = small[(2 + experts_all) * block :][:rank_block]
    else:

        def scatter(values):
            return lax.psum_scatter(values, ("dp", "ctx"), scatter_dimension=0, tiled=True)

        norm_one_grad = scatter(lax.psum(norm_one_part, "mp"))
        norm_two_grad = scatter(lax.psum(norm_two_part, "mp"))
        latent_gain_grad = scatter(lax.psum(latent_gain_part, "mp"))
        router_grad = scatter(router_part.T)

    return (
        result.reshape(seq_count, span_len, D),
        input_grad.reshape(seq_count, span_len, D),
        norm_one_grad,
        query_grad,
        latent_grad,
        latent_gain_grad,
        expand_grad,
        output_grad,
        norm_two_grad,
        router_grad,
        jnp.stack(gate_grads),
        jnp.stack(up_grads),
        jnp.stack(down_grads),
        sboth_grad[:, :shared_cols],
        sboth_grad[:, shared_pad : shared_pad + shared_cols],
        sdown_grad,
    )


def solution(mesh):
    both = ("dp", "ctx")
    tokens = P("dp", "ctx", None)
    in_specs = (
        tokens,
        P(both),
        P(both, "mp"),
        P(both, None),
        P(both),
        P(both, "mp"),
        P("mp", both),
        P(both),
        P(both, None),
        P("mp", both, None),
        P("mp", both, None),
        P("mp", None, both),
        P(both, "mp"),
        P(both, "mp"),
        P("mp", both),
        tokens,
        tokens,
        tokens,
    )
    out_specs = (tokens,) + in_specs[:1] + in_specs[1:15]
    sizes = dict(mesh.shape)

    def per_device(*args):
        return local(sizes, *args)

    return jax.shard_map(
        per_device, mesh=mesh, in_specs=in_specs, out_specs=out_specs, check_vma=False
    )
```

```python
import jax
import jax.numpy as jnp
from jax import lax
from jax.experimental import pallas as pl
from jax.experimental.pallas import tpu as pltpu
from jax.sharding import PartitionSpec as P


D = 2048
QN = 128
QR = 64
VD = 128
KVR = 512
TOP = 6
LANES = 128
EPSILON = 1e-06
LAT, EXPAND, OUTPUT, QUERY, SHARED, DOWN, SDOWN, GATE, UP = "012345678"
ONE, TWO, THREE, FOUR, FIVE = "abcde"
F32 = jnp.float32
BF16 = jnp.bfloat16


def dot_nn(left_in, right_in):
    return lax.dot_general(left_in, right_in, (((1,), (0,)), ((), ())), preferred_element_type=F32)


def dot_tn(left_in, right_in):
    return lax.dot_general(left_in, right_in, (((0,), (0,)), ((), ())), preferred_element_type=F32)


def dot_nt(left_in, right_in):
    return lax.dot_general(left_in, right_in, (((1,), (1,)), ((), ())), preferred_element_type=F32)


def norm_rows(values, gain_vec):
    inverse = lax.rsqrt(jnp.mean(values * values, axis=-1, keepdims=True) + EPSILON)
    normed = values * inverse
    return (normed * gain_vec, normed, inverse)


def norm_back(grad_out, normed, inverse, gain_vec):
    scaled = grad_out * gain_vec
    grad_in = inverse * (scaled - normed * jnp.mean(normed * scaled, axis=-1, keepdims=True))
    return (grad_in, jnp.sum(grad_out * normed, axis=0))


def rotate(values, cosines, sines):
    half_dim = values.shape[-1] // 2
    first_half = values[..., :half_dim]
    second_half = values[..., half_dim:]
    return jnp.concatenate(
        [first_half * cosines - second_half * sines, second_half * cosines + first_half * sines],
        axis=-1,
    )


def bytes_of(*arrays):
    return sum(v.size * v.dtype.itemsize for v in arrays)


def cost(flops, moved, exps=0):
    return pl.CostEstimate(flops=flops, transcendentals=exps, bytes_accessed=moved)


def tile_of(count, parts):
    while parts > 1 and (count % parts or (count // parts) % 16):
        parts -= 1
    return count // parts


def column_blocks(order, values):
    rows, cols = values.shape
    width = cols // 8
    tile = tile_of(rows, 4)

    def body(order_ref, in_ref, out_ref):
        for i in range(8):
            start = pl.multiple_of(order_ref[i] * width, width)
            out_ref[:, i * width : (i + 1) * width] = in_ref[:, pl.ds(start, width)]

    spec = pl.BlockSpec((tile, cols), lambda i, order_ref: (i, 0))
    return pl.pallas_call(
        body,
        out_shape=jax.ShapeDtypeStruct(values.shape, values.dtype),
        grid_spec=pltpu.PrefetchScalarGridSpec(
            num_scalar_prefetch=1, grid=(rows // tile,), in_specs=[spec], out_specs=spec
        ),
        cost_estimate=cost(0, 2 * bytes_of(values)),
    )(order, values)


def row_blocks(order, values):
    rows = values.shape[0] // 8

    def body(order_ref, in_ref, out_ref):
        for i in range(8):
            start = pl.multiple_of(order_ref[i] * rows, rows)
            out_ref[i * rows : (i + 1) * rows, :] = in_ref[pl.ds(start, rows), :]

    spec = pl.BlockSpec(values.shape, lambda i, order_ref: (0, 0))
    return pl.pallas_call(
        body,
        out_shape=jax.ShapeDtypeStruct(values.shape, values.dtype),
        grid_spec=pltpu.PrefetchScalarGridSpec(
            num_scalar_prefetch=1, grid=(1,), in_specs=[spec], out_specs=spec
        ),
        cost_estimate=cost(0, 2 * bytes_of(values)),
    )(order, values)


def place_rows(order, pieces):
    rows, cols = pieces[0].shape
    count = len(pieces)

    def body(order_ref, *refs):
        for i in range(count):
            start = pl.multiple_of(order_ref[i] * rows, rows)
            refs[count][pl.ds(start, rows), :] = refs[i][...]

    return pl.pallas_call(
        body,
        out_shape=jax.ShapeDtypeStruct((count * rows, cols), pieces[0].dtype),
        grid_spec=pltpu.PrefetchScalarGridSpec(
            num_scalar_prefetch=1,
            grid=(1,),
            in_specs=[pl.BlockSpec((rows, cols), lambda i, order_ref: (0, 0))] * count,
            out_specs=pl.BlockSpec((count * rows, cols), lambda i, order_ref: (0, 0)),
        ),
        cost_estimate=cost(0, 2 * bytes_of(*pieces)),
    )(order, *pieces)


def arrivals(group):
    return 0 if group["x_first"] else 1


def add_three(groups, last, total):
    count = len(groups)
    cols = last[0].shape[1]
    axis, size = groups[0]["axis"], groups[0]["size"]
    tile = tile_of(total, 4)
    specs = []
    for g in groups:
        skip = arrivals(g) * (size // tile) if axis == 0 else 0
        side = arrivals(g) if axis == 1 else 0
        specs.append(pl.BlockSpec((tile, cols), lambda i: (i, 0)))
        specs.append(pl.BlockSpec((tile, cols), lambda i, skip=skip, side=side: (i + skip, side)))
        specs.append(pl.BlockSpec((tile, cols), lambda i: (i, 0)))

    def body(*refs):
        for e in range(count):
            held, here, after = (refs[3 * e + k][...].astype(F32) for k in range(3))
            refs[3 * count][e] = held + here + after

    return pl.pallas_call(
        body,
        out_shape=jax.ShapeDtypeStruct((count, total, cols), F32),
        grid=(total // tile,),
        in_specs=specs,
        out_specs=pl.BlockSpec((count, tile, cols), lambda i: (0, i, 0)),
        cost_estimate=cost(3 * count * total * cols, 10 * count * total * cols),
    )(*[v for g, w in zip(groups, last) for v in (g["held"], g["near"], w)])


def add_three_turned(group, last, columns):
    rows, cols = last.shape
    side = arrivals(group)
    spec = pl.BlockSpec((rows, cols), lambda i: (0, 0))

    def body(held_ref, here_ref, last_ref, *out_refs):
        for ref, (start, count) in zip(out_refs, columns):
            part = slice(start, start + count)
            total = held_ref[:, part].astype(F32) + here_ref[:, part].astype(F32)
            ref[...] = (total + last_ref[:, part].astype(F32)).T

    return pl.pallas_call(
        body,
        out_shape=[jax.ShapeDtypeStruct((n, rows), F32) for _, n in columns],
        grid=(1,),
        in_specs=[spec, pl.BlockSpec((rows, cols), lambda i: (side, 0)), spec],
        out_specs=[pl.BlockSpec((n, rows), lambda i: (0, 0)) for _, n in columns],
        cost_estimate=cost(3 * rows * cols, 10 * rows * cols),
    )(group["held"], group["near"], last)


def join_columns(pieces):
    rows, width = pieces[0].shape
    count = len(pieces)
    tile = tile_of(rows, max(2, bytes_of(*pieces) >> 20))

    def body(*refs):
        for i in range(count):
            refs[count][:, i * width : (i + 1) * width] = refs[i][...]

    return pl.pallas_call(
        body,
        out_shape=jax.ShapeDtypeStruct((rows, count * width), pieces[0].dtype),
        grid=(rows // tile,),
        in_specs=[pl.BlockSpec((tile, width), lambda i: (i, 0))] * count,
        out_specs=pl.BlockSpec((tile, count * width), lambda i: (i, 0)),
        cost_estimate=cost(0, 2 * bytes_of(*pieces)),
    )(*pieces)


def join_rows(pieces, count, joined=None):
    experts, rows, cols = pieces[0].shape
    given = len(pieces)
    tile = tile_of(rows, max(2, bytes_of(*pieces) >> 20))
    shape = jax.ShapeDtypeStruct((count, rows, cols), pieces[0].dtype)
    if joined is None:
        places = [i for i in range(count) if given == count or i % 4 != 2]

        def body(*refs):
            for e in range(experts):
                for ref, place in zip(refs, places):
                    refs[given + e][place] = ref[e]

        out = pl.pallas_call(
            body,
            out_shape=[shape] * experts,
            grid=(rows // tile,),
            in_specs=[pl.BlockSpec((experts, tile, cols), lambda i: (0, i, 0))] * given,
            out_specs=[pl.BlockSpec((count, tile, cols), lambda i: (0, i, 0))] * experts,
            cost_estimate=cost(0, 2 * bytes_of(*pieces)),
        )(*pieces)
        return [v.reshape(count * rows, cols) for v in out]
    whole = [v.reshape(given, count // given, rows, cols) for v in joined]

    def fill(*refs):
        for e in range(experts):
            for i in range(given):
                refs[given + experts + e][i, 0] = refs[i][e]

    out = pl.pallas_call(
        fill,
        out_shape=[jax.ShapeDtypeStruct(v.shape, v.dtype) for v in whole],
        grid=(rows // tile,),
        in_specs=[pl.BlockSpec((experts, tile, cols), lambda i: (0, i, 0))] * given
        + [pl.BlockSpec(memory_space=pl.ANY)] * experts,
        out_specs=[pl.BlockSpec((given, 1, tile, cols), lambda i: (0, 2, i, 0))] * experts,
        input_output_aliases={given + e: e for e in range(experts)},
        cost_estimate=cost(0, 2 * bytes_of(*pieces)),
    )(*pieces, *whole)
    return [v.reshape(count * rows, cols) for v in out]


def pick_of(head, heads):
    half = QR // 2
    row = lax.broadcasted_iota(jnp.int32, (QR, heads * QR), 0)
    lane = lax.broadcasted_iota(jnp.int32, (QR, heads * QR), 1)
    place = (row // half) * (heads * half) + head * half + row % half
    return jnp.where(lane == place, 1.0, 0.0).astype(BF16)


def attend(plain, turned, pairs, rope, query_pos, key_pos, seqs, heads):
    span = plain.shape[0] // seqs
    keys = pairs.shape[0] // seqs
    scale = (QN + QR) ** (-0.5)
    rope_cols = heads * QR

    def body(plain_ref, turned_ref, pairs_ref, rope_ref, qpos_ref, kpos_ref, probs_ref, out_ref):
        turned_own = dot_nt(turned_ref[...], pick_of(pl.program_id(1), heads)).astype(BF16)
        logits = dot_nt(plain_ref[...], pairs_ref[:, :QN]) + dot_nt(turned_own, rope_ref[...])
        seen = qpos_ref[...] >= kpos_ref[...]
        exps = jnp.where(seen, jnp.exp(logits * scale), 0.0)
        probs = (exps / jnp.sum(exps, axis=-1, keepdims=True)).astype(BF16)
        probs_ref[0] = probs
        out_ref[...] = dot_nn(probs, pairs_ref[:, QN:]).astype(BF16)

    return pl.pallas_call(
        body,
        out_shape=(
            jax.ShapeDtypeStruct((seqs * heads, span, keys), BF16),
            jax.ShapeDtypeStruct((seqs * span, heads * VD), BF16),
        ),
        grid=(seqs, heads),
        in_specs=[
            pl.BlockSpec((span, QN), lambda s, h: (s, h)),
            pl.BlockSpec((span, rope_cols), lambda s, h: (s, 0)),
            pl.BlockSpec((keys, QN + VD), lambda s, h: (s, h)),
            pl.BlockSpec((keys, QR), lambda s, h: (s, 0)),
            pl.BlockSpec((span, 1), lambda s, h: (0, 0)),
            pl.BlockSpec((1, keys), lambda s, h: (0, 0)),
        ],
        out_specs=(
            pl.BlockSpec((1, span, keys), lambda s, h: (s * heads + h, 0, 0)),
            pl.BlockSpec((span, VD), lambda s, h: (s, h)),
        ),
        cost_estimate=cost(
            2 * seqs * heads * span * keys * (QN + rope_cols + VD),
            bytes_of(plain, turned, pairs) + 2 * seqs * heads * span * keys,
            seqs * heads * span * keys,
        ),
    )(plain, turned, pairs, rope, query_pos[:, None], key_pos[None, :])


def attend_back(plain, turned, pairs, rope, probs, grad_heads, seqs, heads):
    span = plain.shape[0] // seqs
    keys = pairs.shape[0] // seqs
    scale = (QN + QR) ** (-0.5)
    rope_cols = heads * QR

    def body(
        plain_ref, turned_ref, pairs_ref, rope_ref, probs_ref, grad_ref,
        dplain_ref, dturned_ref, dpairs_ref, drope_ref,
    ):
        head = pl.program_id(1)
        pick = pick_of(head, heads)
        turned_own = dot_nt(turned_ref[...], pick).astype(BF16)
        probs_low = probs_ref[0]
        probs_f = probs_low.astype(F32)
        grad = grad_ref[...]
        grad_probs = dot_nt(grad, pairs_ref[:, QN:])
        delta = jnp.sum(probs_f * grad_probs, axis=-1, keepdims=True)
        grad_logits = (probs_f * (grad_probs - delta) * scale).astype(BF16)
        dplain_ref[...] = dot_nn(grad_logits, pairs_ref[:, :QN]).astype(BF16)
        dpairs_ref[:, QN:] = dot_tn(probs_low, grad).astype(BF16)
        dpairs_ref[:, :QN] = dot_tn(grad_logits, plain_ref[...]).astype(BF16)
        turned_part = dot_nn(dot_nn(grad_logits, rope_ref[...]).astype(BF16), pick)
        rope_part = dot_tn(grad_logits, turned_own)

        @pl.when(head == 0)
        def _():
            dturned_ref[...] = turned_part
            drope_ref[...] = rope_part

        @pl.when(head > 0)
        def _():
            dturned_ref[...] += turned_part
            drope_ref[...] += rope_part

    return pl.pallas_call(
        body,
        out_shape=(
            jax.ShapeDtypeStruct(plain.shape, BF16),
            jax.ShapeDtypeStruct(turned.shape, F32),
            jax.ShapeDtypeStruct(pairs.shape, BF16),
            jax.ShapeDtypeStruct(rope.shape, F32),
        ),
        grid=(seqs, heads),
        in_specs=[
            pl.BlockSpec((span, QN), lambda s, h: (s, h)),
            pl.BlockSpec((span, rope_cols), lambda s, h: (s, 0)),
            pl.BlockSpec((keys, QN + VD), lambda s, h: (s, h)),
            pl.BlockSpec((keys, QR), lambda s, h: (s, 0)),
            pl.BlockSpec((1, span, keys), lambda s, h: (s * heads + h, 0, 0)),
            pl.BlockSpec((span, VD), lambda s, h: (s, h)),
        ],
        out_specs=(
            pl.BlockSpec((span, QN), lambda s, h: (s, h)),
            pl.BlockSpec((span, rope_cols), lambda s, h: (s, 0)),
            pl.BlockSpec((keys, QN + VD), lambda s, h: (s, h)),
            pl.BlockSpec((keys, QR), lambda s, h: (s, 0)),
        ),
        cost_estimate=cost(
            2 * seqs * heads * span * keys * (2 * QN + 2 * VD + 2 * QR),
            2 * bytes_of(plain, turned, pairs) + bytes_of(probs),
        ),
    )(plain, turned, pairs, rope, probs, grad_heads)


def pad_cols(values, width):
    return jnp.pad(values, ((0, 0), (0, width - values.shape[1])))


def up_to(count, step):
    return -(-count // step) * step


class Plan:
    def __init__(self, sizes):
        self.dp = sizes["dp"]
        self.ctx = sizes["ctx"]
        self.fast = self.dp == 4 and self.ctx == 2
        if self.fast:
            me = lax.axis_index("dp") * 2 + lax.axis_index("ctx")
            ids = jnp.arange(8, dtype=jnp.int32)
            y, core, x = (ids >> 1) & 1, ids >> 2, (ids ^ (ids >> 1)) & 1
            self.order = ((4 * y + 2 * core + x) ^ me).astype(jnp.int32)
            apart = ids ^ me
            y, core, x = apart >> 2, (apart >> 1) & 1, apart & 1
            self.inverse = (4 * core + x + y * (3 - 2 * x)).astype(jnp.int32)

    @staticmethod
    def over_core(values):
        return lax.ppermute(values, "dp", [(i, i ^ 1) for i in range(4)])

    @staticmethod
    def over_y(values):
        return lax.ppermute(values, "dp", [(i, i ^ 2) for i in range(4)])

    @staticmethod
    def over_x(values):
        return lax.ppermute(values, "ctx", [(0, 1), (1, 0)])

    def tie(self, values, *after):
        return lax.optimization_barrier((values, after))[0] if self.fast else values

    def to_own(self, values):
        return column_blocks(self.order, values) if self.fast else values

    def to_natural(self, values):
        return column_blocks(self.inverse, values) if self.fast else values

    def spread(self, shard):
        if not self.fast:
            return ()
        return (self.over_x(shard), self.over_y(shard))

    def collect(self, name, shard, near, axis, x_last, *after):
        if not self.fast:
            full = lax.all_gather(shard, ("dp", "ctx"), axis=axis, tiled=True)
            return (list(full), lambda *after: list(full)) if shard.ndim == 3 else full
        from_x, from_y = near
        from_xy = self.over_x(from_y) if x_last else self.over_y(from_x)
        own = [shard, from_x, from_xy, from_y]
        if shard.ndim == 3:
            early = self.tie([shard, from_x, from_y], *after)
            early = early + [self.over_core(v) for v in early]
            joined = join_rows(early, 8)

            def rest(*after):
                late = self.tie(from_xy, joined, *after)
                late = [late, self.over_core(late)]
                return join_rows(late, 8, joined)

            return joined, rest
        own[2] = self.tie(from_xy, *after)
        pieces = own + [self.over_core(v) for v in own]
        if name == EXPAND:
            return place_rows(self.order, pieces)
        if axis == 0:
            return join_rows([v[None] for v in pieces], 8)[0]
        return join_columns(pieces)

    def over(self, values, first, x_first):
        return self.over_x(values) if first == x_first else self.over_y(values)

    def begin(self, name, left_in, right_in, size, axis, x_first):
        if not self.fast:
            return self.begin_given(name, dot_tn(left_in, right_in).astype(BF16), size, axis, x_first)
        half = 4 * size

        def part(a, b):
            if axis == 0:
                return dot_tn(left_in[:, a:b], right_in)
            return dot_tn(left_in, right_in[:, a:b])

        sent = self.over_core(part(half, 2 * half).astype(BF16))
        held = (part(0, half) + sent.astype(F32)).astype(BF16)
        return {"held": held, "x_first": x_first, "name": name, "size": size, "axis": axis}

    def cut(self, group, name, i, count=1):
        size = group["size"]
        return lax.slice_in_dim(group[name], i * size, (i + count) * size, axis=group["axis"])

    def begin_given(self, name, whole, size, axis, x_first):
        if not self.fast:
            held = lax.psum_scatter(whole, ("dp", "ctx"), scatter_dimension=axis, tiled=True)
        else:
            sent = self.over_core(lax.slice_in_dim(whole, 4 * size, 8 * size, axis=axis))
            held = lax.slice_in_dim(whole, 0, 4 * size, axis=axis).astype(F32)
            held = (held + sent.astype(F32)).astype(BF16)
        return {"held": held, "x_first": x_first, "name": name, "size": size, "axis": axis}

    def first(self, groups):
        if not self.fast:
            return
        for g in groups:
            both = self.cut(g, "held", 1 if g["x_first"] else 2, 2)
            g["near"] = self.over(both, True, g["x_first"])

    def second(self, groups, *after):
        if not self.fast:
            return
        near = self.tie([g["near"] for g in groups], *after)
        for g, v in zip(groups, near):
            g["near"] = v
            kept = self.cut(g, "held", 3 if g["x_first"] else 1).astype(F32)
            there = self.cut(g, "near", 1 if g["x_first"] else 0).astype(F32)
            g["last"] = self.over((kept + there).astype(BF16), False, g["x_first"])

    def finish(self, groups, rows, *after):
        if not self.fast:
            return jnp.stack([g["held"][:rows].astype(F32) for g in groups])
        last = self.tie([g["last"] for g in groups], *after)
        return add_three(groups, last, rows)

    def finish_turned(self, group, columns, *after):
        if not self.fast:
            return [group["held"][:, a : a + n].astype(F32) for a, n in columns]
        last = self.tie(group["last"], *after)
        return [v.T for v in add_three_turned(group, last, columns)]


def scatter_mp(values, n_mp, direct, tie):
    if not direct:
        return lax.psum_scatter(values, "mp", scatter_dimension=0, tiled=True).astype(F32)
    share = values.shape[0] // n_mp
    me = lax.axis_index("mp")

    def part(i):
        return lax.dynamic_slice_in_dim(values, (i % n_mp) * share, share, axis=0)

    arrived = []
    for step in range(1, n_mp):
        path = [(i, (i + step) % n_mp) for i in range(n_mp)]
        arrived.append(lax.ppermute(part(me + step), "mp", path))
    return sum((v.astype(F32) for v in tie(arrived)), part(me).astype(F32))


def gather_mp(values, n_mp, direct, tie):
    if not direct:
        return lax.all_gather(values, "mp", axis=0, tiled=True)
    share = values.shape[0]
    me = lax.axis_index("mp")
    others = [values]
    for step in range(1, n_mp):
        path = [(i, (i + step) % n_mp) for i in range(n_mp)]
        others.append(lax.ppermute(values, "mp", path))
    whole = jnp.zeros((n_mp * share,) + values.shape[1:], values.dtype)
    for step, other in enumerate(tie(others)):
        whole = lax.dynamic_update_slice_in_dim(
            whole, other, ((me - step) % n_mp) * share, axis=0
        )
    return whole


def sum_mp(values, n_mp):
    total = values
    for step in range(1, n_mp):
        path = [(i, (i + step) % n_mp) for i in range(n_mp)]
        total = total + lax.ppermute(values, "mp", path)
    return total


def local(
    sizes,
    block_input,
    norm_one_gain,
    query_weight,
    latent_weight,
    latent_gain,
    expand_weight,
    output_weight,
    norm_two_gain,
    router_weight,
    expert_gate,
    expert_up,
    expert_down,
    shared_gate,
    shared_up,
    shared_down,
    routes,
    route_slots,
    cotangent,
):
    plan = Plan(sizes)
    fast = plan.fast
    n_mp = sizes["mp"]
    mp_index = lax.axis_index("mp")
    seq_count, span_len = block_input.shape[0], block_input.shape[1]
    rows = seq_count * span_len
    shard_rows = rows // n_mp
    head_dim = QN + QR
    q_cols = query_weight.shape[1]
    local_heads = q_cols // head_dim
    experts_here = expert_gate.shape[0]
    experts_all = router_weight.shape[1]
    hidden = expert_gate.shape[2]
    shared_cols = shared_gate.shape[1]
    shared_pad = up_to(shared_cols, 2 * LANES)
    block = norm_one_gain.shape[0]
    rank_block = expand_weight.shape[0]

    half_dim = QR // 2
    both_halves = local_heads * half_dim

    if fast:
        gains = jnp.concatenate([norm_one_gain, norm_two_gain, latent_gain]).astype(F32)[None]
        gains_x = plan.over_x(gains)
        gains = jnp.concatenate([gains, gains_x], axis=0)
        gains_y = plan.over_y(gains)
        gains = jnp.concatenate([gains, gains_y[1:], gains_y[:1]], axis=0)
        gains_core = plan.over_core(gains)
        gains = jnp.concatenate([gains, gains_core], axis=0)
        gain_one = gains[:, :block].reshape(8 * block)
        gain_two = gains[:, block : 2 * block].reshape(8 * block)
        rank_rel = gains[:, 2 * block :]
        place = (plan.inverse[:, None] == jnp.arange(8, dtype=jnp.int32)[None, :]).astype(F32)
        gain_latent = jnp.sum(place[:, :, None] * rank_rel[None, :, :], axis=1).reshape(KVR)
    latent_cols = KVR + QR
    latent_shard = jnp.concatenate([latent_weight, router_weight], axis=1)
    latent_near = plan.spread(latent_shard)
    expand_near = plan.spread(expand_weight)
    output_near = plan.spread(output_weight)
    query_weight = plan.tie(query_weight, *latent_near)
    by_head = query_weight.reshape(block, local_heads, head_dim)
    query_shard = jnp.concatenate(
        [
            by_head[:, :, :QN].reshape(block, local_heads * QN),
            by_head[:, :, QN : QN + half_dim].reshape(block, both_halves),
            by_head[:, :, QN + half_dim :].reshape(block, both_halves),
        ],
        axis=1,
    )
    query_near = plan.spread(query_shard)
    latent_router = plan.collect(LAT, latent_shard, latent_near, 0, True)
    latent_full = latent_router[:, :latent_cols]
    router_full = latent_router[:, latent_cols:]
    if not fast:
        gain_one = lax.all_gather(norm_one_gain, ("dp", "ctx"), tiled=True).astype(F32)
        gain_two = lax.all_gather(norm_two_gain, ("dp", "ctx"), tiled=True).astype(F32)
        gain_latent = lax.all_gather(latent_gain, ("dp", "ctx"), tiled=True).astype(F32)

    ctx_index = lax.axis_index("ctx")
    frequencies = 10000.0 ** (-jnp.arange(half_dim, dtype=F32) / half_dim)
    steps = jnp.arange(span_len, dtype=jnp.int32)
    query_pos = ctx_index * span_len + steps
    angles = jnp.tile(query_pos.astype(F32)[:, None] * frequencies[None, :], (seq_count, 1))
    cosines = jnp.cos(angles)
    sines = jnp.sin(angles)
    lanes = jnp.arange(both_halves, dtype=jnp.int32) % half_dim
    all_frequencies = 10000.0 ** (-lanes.astype(F32) / half_dim)
    all_angles = jnp.tile(query_pos.astype(F32), seq_count)[:, None] * all_frequencies[None, :]
    cos_heads = jnp.cos(all_angles)
    sin_heads = jnp.sin(all_angles)

    row_start = mp_index * shard_rows

    def own_rows(values):
        return lax.dynamic_slice_in_dim(values, row_start, shard_rows, axis=0)

    x_low = plan.to_own(block_input.reshape(rows, D))
    x_own = own_rows(x_low).astype(F32)
    h_one = norm_rows(x_low.astype(F32), gain_one)[0].astype(BF16)
    latent = dot_nn(h_one, latent_router)[:, :latent_cols]
    comp_f = norm_rows(latent[:, :KVR], gain_latent)[0]
    key_rope = rotate(latent[:, KVR:], cosines, sines)
    shared_kv = jnp.concatenate([comp_f, key_rope], axis=1).astype(BF16)

    shared_kv = shared_kv.reshape(seq_count, span_len, KVR + QR)
    if plan.ctx == 2:
        other_kv = plan.over_x(shared_kv)
        kv_all = jnp.concatenate([shared_kv, other_kv], axis=1)
        key_pos = jnp.concatenate([query_pos, (1 - ctx_index) * span_len + steps])
    else:
        kv_all = lax.all_gather(shared_kv, "ctx", axis=1, tiled=True)
        key_pos = jnp.arange(plan.ctx * span_len, dtype=jnp.int32)
    down_shards = [expert_down[e] for e in range(experts_here)]
    down_shards = plan.tie(down_shards, shared_kv)
    down_near = [plan.spread(v) for v in down_shards]
    gate_shard = plan.tie(expert_gate, shared_kv)
    gate_near = plan.spread(gate_shard)

    query_near, expand_near, output_near = (
        plan.tie(v, shared_kv) for v in (query_near, expand_near, output_near)
    )
    query_full = plan.collect(QUERY, query_shard, query_near, 0, False)
    expand_full = plan.collect(EXPAND, expand_weight, expand_near, 0, False)
    output_full = plan.collect(OUTPUT, output_weight, output_near, 1, True)
    seq_len = key_pos.shape[0]
    comp_all = kv_all[..., :KVR].reshape(seq_count * seq_len, KVR)
    rope_all = kv_all[..., KVR:].reshape(seq_count * seq_len, QR)
    q_raw = dot_nn(h_one, query_full)
    plain_cols = local_heads * QN
    plain = q_raw[:, :plain_cols].astype(BF16)
    first = q_raw[:, plain_cols : plain_cols + both_halves]
    second = q_raw[:, plain_cols + both_halves :]
    turned = jnp.concatenate(
        [first * cos_heads - second * sin_heads, second * cos_heads + first * sin_heads], axis=1
    ).astype(BF16)
    pairs = dot_nn(comp_all, expand_full).astype(BF16)
    probs, heads_flat = attend(
        plain, turned, pairs, rope_all, query_pos, key_pos, seq_count, local_heads
    )
    attn_part = dot_nn(heads_flat, output_full).astype(BF16)
    attn_sum = lax.psum_scatter(attn_part, "mp", scatter_dimension=0, tiled=True)

    cotangent, route_rows, slot_rows = plan.tie(
        (cotangent, routes.reshape(rows, TOP), route_slots.reshape(rows, TOP)), attn_part
    )
    g_low = plan.to_own(cotangent.reshape(rows, D))
    g_own = own_rows(g_low).astype(F32)
    slot_ids = jnp.arange(rows, dtype=jnp.int32)
    hits = []
    for e in range(experts_here):
        named = route_rows == mp_index * experts_here + e
        slot = jnp.sum(jnp.where(named, slot_rows + 1, 0), axis=-1) - 1
        hits.append(slot[:, None] == slot_ids[None, :])
    one_hot = [v.astype(BF16) for v in hits]
    both_hot = jnp.concatenate(one_hot, axis=1)
    g_slots = [dot_tn(v, g_low).astype(BF16) for v in one_hot]
    down_near = [plan.tie(v, attn_part) for v in down_near]
    down_full = [plan.collect(DOWN, down_shards[0], down_near[0], 1, True, *g_slots)]
    act_back = [dot_nt(g_slots[0], down_full[0]).astype(BF16)]
    attn_sum = plan.tie(attn_sum, act_back, *g_slots)
    up_shard = plan.tie(expert_up, attn_part)
    up_near = plan.spread(up_shard)
    shared_gate, shared_up, shared_down = plan.tie((shared_gate, shared_up, shared_down), *g_slots)
    shared_shard = jnp.concatenate(
        [pad_cols(shared_gate, shared_pad), pad_cols(shared_up, shared_pad)], axis=1
    )
    sdown_shard = jnp.pad(shared_down, ((0, shared_pad - shared_cols), (0, 0)))
    shared_near = plan.spread(shared_shard)
    sdown_near = plan.spread(sdown_shard)

    mixed = x_own + attn_sum.astype(F32)
    h_two_f, normed_two, inverse_two = norm_rows(mixed, gain_two)
    h_two_own = h_two_f.astype(BF16)
    h_two = lax.all_gather(h_two_own, "mp", axis=0, tiled=True)

    gate_near = plan.tie(gate_near, h_two_own)
    gate_joined, gate_rest = plan.collect(GATE, gate_shard, gate_near, 1, True)
    up_near = plan.tie(up_near, gate_joined)
    up_joined, up_rest = plan.collect(UP, up_shard, up_near, 1, False)
    after = up_joined
    for e in range(1, experts_here):
        full = plan.collect(DOWN, down_shards[e], down_near[e], 1, e % 2 == 0, after)
        down_full.append(full)
        act_back.append(dot_nt(g_slots[e], full).astype(BF16))
        after = act_back[e]
    gate_full = gate_rest(after)

    dispatched = [dot_tn(v, h_two).astype(BF16) for v in one_hot]
    gate_all = plan.tie([dot_nn(dispatched[e], gate_full[e]) for e in range(experts_here)])
    up_full = up_rest(gate_all)
    router_exp = jnp.exp(dot_nn(h_two, router_full))
    router_probs = router_exp / jnp.sum(router_exp, axis=-1, keepdims=True)
    probs_here = lax.dynamic_slice_in_dim(router_probs, mp_index * experts_here, experts_here, 1)
    slot_gate = [
        jnp.sum(jnp.where(hits[e], probs_here[:, e : e + 1], 0.0), axis=0)
        for e in range(experts_here)
    ]
    grad_gates, grad_ups, act_gated, slot_grads = [], [], [], []
    for e in range(experts_here):
        gate_vals = gate_all[e]
        up_vals = dot_nn(dispatched[e], up_full[e])
        sig = jax.nn.sigmoid(gate_vals)
        act = gate_vals * sig * up_vals
        gated = slot_gate[e][:, None]
        back = act_back[e].astype(F32)
        slot_grads.append(jnp.sum(back * act, axis=-1))
        back = back * gated
        grad_gate = (back * up_vals * sig * (1.0 + gate_vals * (1.0 - sig))).astype(BF16)
        grad_up = (back * gate_vals * sig).astype(BF16)
        grad_gate, grad_up, act = plan.tie((grad_gate, grad_up, (act * gated).astype(BF16)))
        grad_gates.append(grad_gate)
        grad_ups.append(grad_up)
        act_gated.append(act)


    shared_near, sdown_near = plan.tie((shared_near, sdown_near), h_two_own)
    shared_full = plan.collect(SHARED, shared_shard, shared_near, 0, False, act_gated)
    sdown_full = plan.collect(SDOWN, sdown_shard, sdown_near, 1, True, shared_full)
    shared_back = dot_nt(g_low, sdown_full)
    shared_vals = dot_nn(h_two, shared_full)
    shared_a = shared_vals[:, :shared_pad]
    shared_b = shared_vals[:, shared_pad:]
    shared_sig = jax.nn.sigmoid(shared_a)
    shared_act = (shared_a * shared_sig * shared_b).astype(BF16)
    grad_shared_gate = shared_back * shared_b * shared_sig * (1.0 + shared_a * (1.0 - shared_sig))
    grad_shared_up = shared_back * shared_a * shared_sig
    grad_shared = jnp.concatenate([grad_shared_gate, grad_shared_up], axis=1).astype(BF16)

    grad_slots = []
    for e in range(experts_here):
        grad_slot = dot_nt(grad_gates[e], gate_full[e]) + dot_nt(grad_ups[e], up_full[e])
        grad_slots.append(grad_slot.astype(BF16))
    grad_h_two = dot_nn(both_hot, jnp.concatenate(grad_slots, axis=0)) + dot_nt(
        grad_shared, shared_full
    )
    expert_ids = jnp.arange(LANES, dtype=jnp.int32)
    grad_probs_part = jnp.zeros((rows, LANES), F32)
    for e in range(experts_here):
        of_token = jnp.sum(jnp.where(hits[e], slot_grads[e][None, :], 0.0), axis=1)
        grad_probs_part = grad_probs_part + jnp.where(
            expert_ids[None, :] == mp_index * experts_here + e, of_token[:, None], 0.0
        )
    back_part = jnp.concatenate([grad_h_two.astype(BF16), grad_probs_part.astype(BF16)], axis=1)
    back_sum = lax.psum_scatter(back_part, "mp", scatter_dimension=0, tiled=True).astype(F32)

    acts, slots_g, acts_s, g_late, h_late, shared_late = plan.tie(
        (act_gated, g_slots, shared_act, g_low, h_two, grad_shared), back_part
    )
    sums_one = [
        plan.begin(ONE, h_late, shared_late, block, 0, False),
        plan.begin(ONE, acts_s, g_late, block, 1, True),
    ] + [
        plan.begin(ONE, acts[e], slots_g[e], block, 1, e % 2 == 0)
        for e in range(experts_here)
    ]
    plan.first(sums_one)
    back_sum = plan.tie(back_sum, *[g["held"] for g in sums_one])

    probs_own = own_rows(router_probs)
    grad_probs = back_sum[:, D : D + experts_all]
    grad_logits = (
        probs_own * (grad_probs - jnp.sum(probs_own * grad_probs, axis=-1, keepdims=True))
    ).astype(BF16)
    grad_two = back_sum[:, :D] + dot_nt(grad_logits, router_full)
    grad_norm, norm_two_part = norm_back(grad_two, normed_two, inverse_two, gain_two)
    grad_mixed = g_own + grad_norm
    mixed_part = jnp.concatenate([grad_mixed.astype(BF16), pad_cols(grad_logits, LANES)], axis=1)
    mixed_all = lax.all_gather(mixed_part, "mp", axis=0, tiled=True)

    acts_out, shared_act_out = plan.tie((act_gated, shared_act), mixed_part)
    expert_out = [dot_nn(acts_out[e], down_full[e]).astype(BF16) for e in range(experts_here)]
    ff_part = dot_nn(both_hot, jnp.concatenate(expert_out, axis=0)) + dot_nn(
        shared_act_out, sdown_full
    )
    ff_part = ff_part.astype(BF16)
    ff_sum = lax.psum_scatter(ff_part, "mp", scatter_dimension=0, tiled=True).astype(F32)


    sent_rows, gates_late = plan.tie((dispatched, grad_gates), mixed_part)
    sums_two = [
        plan.begin(TWO, sent_rows[e], gates_late[e], block, 0, e % 2 == 0)
        for e in range(experts_here)
    ]
    plan.first(sums_two)
    mixed_all = plan.tie(mixed_all, *[g["held"] for g in sums_two])

    grad_low = mixed_all[:, :D]
    grad_heads = dot_nt(grad_low, output_full).astype(BF16)
    dplain, dturned, grad_pairs, grad_rope = attend_back(
        plain, turned, pairs, rope_all, probs, grad_heads, seq_count, local_heads
    )
    back_first = dturned[:, :both_halves]
    back_second = dturned[:, both_halves:]
    grad_q_raw = jnp.concatenate(
        [
            dplain,
            (back_first * cos_heads + back_second * sin_heads).astype(BF16),
            (back_second * cos_heads - back_first * sin_heads).astype(BF16),
        ],
        axis=1,
    )
    query_part = dot_nt(grad_q_raw, query_full).astype(BF16)
    grad_one = lax.psum_scatter(query_part, "mp", scatter_dimension=0, tiled=True).astype(F32)
    grad_comp = dot_nt(grad_pairs, expand_full).reshape(seq_count, seq_len, KVR)
    grad_rope = grad_rope.reshape(seq_count, seq_len, QR)
    grad_kv = jnp.concatenate([grad_comp, grad_rope], axis=-1)
    if plan.ctx == 2:
        to_other = grad_kv[:, span_len:].astype(BF16)
        from_other = plan.over_x(to_other)
        grad_kv = grad_kv[:, :span_len] + from_other.astype(F32)
    else:
        to_other = ()
        grad_kv = grad_kv.reshape(seq_count, plan.ctx, span_len, KVR + QR).transpose(1, 0, 2, 3)
        grad_kv = grad_kv.reshape(plan.ctx * rows, KVR + QR).astype(BF16)
        grad_kv = lax.psum_scatter(grad_kv, "ctx", scatter_dimension=0, tiled=True)
    sent_late, ups_late = plan.tie((dispatched, grad_ups), query_part, to_other)
    plan.second(sums_one, query_part, to_other)
    plan.second(sums_two, query_part, to_other)
    sums_three = [
        plan.begin(THREE, sent_late[e], ups_late[e], block, 0, e % 2 == 1)
        for e in range(experts_here)
    ]
    plan.first(sums_three)
    grad_kv = scatter_mp(
        grad_kv.reshape(rows, KVR + QR).astype(BF16),
        n_mp,
        fast,
        lambda values: plan.tie(values, *[g["held"] for g in sums_three]),
    )
    _, comp_normed, comp_inverse = norm_rows(own_rows(latent)[:, :KVR], gain_latent)
    grad_comp_in, latent_gain_part = norm_back(
        grad_kv[:, :KVR], comp_normed, comp_inverse, gain_latent
    )
    grad_latent = jnp.concatenate(
        [grad_comp_in, rotate(grad_kv[:, KVR:], own_rows(cosines), -own_rows(sines))], axis=1
    ).astype(BF16)
    grad_one = grad_one + dot_nt(grad_latent, latent_full)
    _, normed_one, inverse_one = norm_rows(x_own, gain_one)
    grad_tokens, norm_one_part = norm_back(grad_one, normed_one, inverse_one, gain_one)
    input_own = plan.to_natural((grad_mixed + grad_tokens).astype(BF16))
    input_grad = lax.all_gather(input_own, "mp", axis=0, tiled=True)

    result_own = plan.to_natural((mixed + ff_sum).astype(BF16))
    result_own = plan.tie(result_own, mixed_all)
    result = lax.all_gather(result_own, "mp", axis=0, tiled=True)

    h_tail, heads_tail, low_tail, q_tail, comp_tail, pairs_tail = plan.tie(
        (h_one, heads_flat, grad_low, grad_q_raw, comp_all, grad_pairs), input_own
    )
    sums_four = [
        plan.begin(FOUR, heads_tail, low_tail, block, 1, True),
        plan.begin(FOUR, h_tail, q_tail, block, 0, False),
    ]
    expand_whole = dot_tn(comp_tail, pairs_tail).astype(BF16)
    if fast:
        expand_whole = row_blocks(plan.order, expand_whole)
    sums_four.append(plan.begin_given(FOUR, expand_whole, rank_block, 0, True))
    plan.first(sums_four)
    held_four = [g["held"] for g in sums_four]
    plan.second(sums_three)
    sgate_grad, sup_grad = plan.finish_turned(
        sums_one[0], [(0, shared_cols), (shared_pad, shared_cols)], held_four
    )
    sdown_grad = plan.finish(sums_one[1:2], shared_cols, held_four)[0]
    down_grads = plan.finish(sums_one[2:], hidden, held_four)
    gate_grads = plan.finish(sums_two, block, held_four)
    latent_all = gather_mp(grad_latent, n_mp, fast, lambda values: plan.tie(values, held_four))
    plan.second(sums_four)
    sums_five = [plan.begin(FIVE, h_tail, latent_all, block, 0, False)]
    plan.first(sums_five)
    plan.second(sums_five)
    up_grads = plan.finish(sums_three, block, latent_all)
    output_grad, query_grad, expand_grad = (
        plan.finish([g], n, latent_all)[0]
        for g, n in zip(sums_four, (output_weight.shape[0], block, rank_block))
    )
    (latent_grad,) = plan.finish_turned(sums_five[0], [(0, latent_cols)])
    query_grad = jnp.concatenate(
        [
            query_grad[:, :plain_cols].reshape(block, local_heads, QN),
            query_grad[:, plain_cols:][:, :both_halves].reshape(block, local_heads, half_dim),
            query_grad[:, plain_cols + both_halves :].reshape(block, local_heads, half_dim),
        ],
        axis=2,
    ).reshape(block, q_cols)

    router_part = dot_tn(mixed_all[:, D : D + experts_all], h_two)
    if fast:
        to_rel = (plan.order[:, None] == jnp.arange(8, dtype=jnp.int32)[None, :]).astype(F32)
        latent_rel = jnp.sum(
            to_rel[:, :, None] * latent_gain_part.reshape(1, 8, rank_block), axis=1
        )
        router_once = jnp.where(mp_index == 0, router_part, 0.0)
        router_rel = router_once.reshape(experts_all, 8, block).transpose(1, 0, 2)
        small = jnp.concatenate(
            [
                norm_one_part.reshape(8, block),
                norm_two_part.reshape(8, block),
                router_rel.reshape(8, experts_all * block),
                pad_cols(latent_rel, LANES),
            ],
            axis=1,
        )
        small = small[:4] + plan.over_core(small[4:])
        from_y = plan.over_y(small[2:])
        small = small[:2] + jnp.concatenate([from_y[1:], from_y[:1]], axis=0)
        small = small[:1] + plan.over_x(small[1:])
        small = sum_mp(small, n_mp)[0]
        norm_one_grad = small[:block]
        norm_two_grad = small[block : 2 * block]
        router_grad = small[2 * block : (2 + experts_all) * block].reshape(experts_all, block).T
        latent_gain_grad = small[(2 + experts_all) * block :][:rank_block]
    else:

        def scatter(values):
            return lax.psum_scatter(values, ("dp", "ctx"), scatter_dimension=0, tiled=True)

        norm_one_grad = scatter(lax.psum(norm_one_part, "mp"))
        norm_two_grad = scatter(lax.psum(norm_two_part, "mp"))
        latent_gain_grad = scatter(lax.psum(latent_gain_part, "mp"))
        router_grad = scatter(router_part.T)

    return (
        result.reshape(seq_count, span_len, D),
        input_grad.reshape(seq_count, span_len, D),
        norm_one_grad,
        query_grad,
        latent_grad,
        latent_gain_grad,
        expand_grad,
        output_grad,
        norm_two_grad,
        router_grad,
        gate_grads,
        up_grads,
        down_grads,
        sgate_grad,
        sup_grad,
        sdown_grad,
    )


def solution(mesh):
    both = ("dp", "ctx")
    tokens = P("dp", "ctx", None)
    in_specs = (
        tokens,
        P(both),
        P(both, "mp"),
        P(both, None),
        P(both),
        P(both, "mp"),
        P("mp", both),
        P(both),
        P(both, None),
        P("mp", both, None),
        P("mp", both, None),
        P("mp", None, both),
        P(both, "mp"),
        P(both, "mp"),
        P("mp", both),
        tokens,
        tokens,
        tokens,
    )
    out_specs = (tokens,) + in_specs[:1] + in_specs[1:15]
    sizes = dict(mesh.shape)

    def per_device(*args):
        return local(sizes, *args)

    return jax.shard_map(
        per_device, mesh=mesh, in_specs=in_specs, out_specs=out_specs, check_vma=False
    )
```

```python
import jax
import jax.numpy as jnp
from jax import lax
from jax.experimental import pallas as pl
from jax.experimental.pallas import tpu as pltpu
from jax.sharding import PartitionSpec as P


D = 2048
QN = 128
QR = 64
VD = 128
KVR = 512
TOP = 6
LANES = 128
EPSILON = 1e-06
LAT, EXPAND, OUTPUT, QUERY, SHARED, DOWN, SDOWN, GATE, UP = "012345678"
ONE, TWO, THREE, FOUR, FIVE = "abcde"
F32 = jnp.float32
BF16 = jnp.bfloat16


def dot_nn(left_in, right_in):
    return lax.dot_general(left_in, right_in, (((1,), (0,)), ((), ())), preferred_element_type=F32)


def dot_tn(left_in, right_in):
    return lax.dot_general(left_in, right_in, (((0,), (0,)), ((), ())), preferred_element_type=F32)


def dot_nt(left_in, right_in):
    return lax.dot_general(left_in, right_in, (((1,), (1,)), ((), ())), preferred_element_type=F32)


def norm_rows(values, gain_vec):
    inverse = lax.rsqrt(jnp.mean(values * values, axis=-1, keepdims=True) + EPSILON)
    normed = values * inverse
    return (normed * gain_vec, normed, inverse)


def norm_back(grad_out, normed, inverse, gain_vec):
    scaled = grad_out * gain_vec
    grad_in = inverse * (scaled - normed * jnp.mean(normed * scaled, axis=-1, keepdims=True))
    return (grad_in, jnp.sum(grad_out * normed, axis=0))


def rotate(values, cosines, sines):
    half_dim = values.shape[-1] // 2
    first_half = values[..., :half_dim]
    second_half = values[..., half_dim:]
    return jnp.concatenate(
        [first_half * cosines - second_half * sines, second_half * cosines + first_half * sines],
        axis=-1,
    )


def bytes_of(*arrays):
    return sum(v.size * v.dtype.itemsize for v in arrays)


def cost(flops, moved, exps=0):
    return pl.CostEstimate(flops=flops, transcendentals=exps, bytes_accessed=moved)


def tile_of(count, parts):
    while parts > 1 and (count % parts or (count // parts) % 16):
        parts -= 1
    return count // parts


def column_blocks(order, values):
    rows, cols = values.shape
    width = cols // 8
    tile = tile_of(rows, 4)

    def body(order_ref, in_ref, out_ref):
        for i in range(8):
            start = pl.multiple_of(order_ref[i] * width, width)
            out_ref[:, i * width : (i + 1) * width] = in_ref[:, pl.ds(start, width)]

    spec = pl.BlockSpec((tile, cols), lambda i, order_ref: (i, 0))
    return pl.pallas_call(
        body,
        out_shape=jax.ShapeDtypeStruct(values.shape, values.dtype),
        grid_spec=pltpu.PrefetchScalarGridSpec(
            num_scalar_prefetch=1, grid=(rows // tile,), in_specs=[spec], out_specs=spec
        ),
        cost_estimate=cost(0, 2 * bytes_of(values)),
    )(order, values)


def row_blocks(order, values):
    rows = values.shape[0] // 8

    def body(order_ref, in_ref, out_ref):
        for i in range(8):
            start = pl.multiple_of(order_ref[i] * rows, rows)
            out_ref[i * rows : (i + 1) * rows, :] = in_ref[pl.ds(start, rows), :]

    spec = pl.BlockSpec(values.shape, lambda i, order_ref: (0, 0))
    return pl.pallas_call(
        body,
        out_shape=jax.ShapeDtypeStruct(values.shape, values.dtype),
        grid_spec=pltpu.PrefetchScalarGridSpec(
            num_scalar_prefetch=1, grid=(1,), in_specs=[spec], out_specs=spec
        ),
        cost_estimate=cost(0, 2 * bytes_of(values)),
    )(order, values)


def place_rows(order, pieces):
    rows, cols = pieces[0].shape
    count = len(pieces)

    def body(order_ref, *refs):
        for i in range(count):
            start = pl.multiple_of(order_ref[i] * rows, rows)
            refs[count][pl.ds(start, rows), :] = refs[i][...]

    return pl.pallas_call(
        body,
        out_shape=jax.ShapeDtypeStruct((count * rows, cols), pieces[0].dtype),
        grid_spec=pltpu.PrefetchScalarGridSpec(
            num_scalar_prefetch=1,
            grid=(1,),
            in_specs=[pl.BlockSpec((rows, cols), lambda i, order_ref: (0, 0))] * count,
            out_specs=pl.BlockSpec((count * rows, cols), lambda i, order_ref: (0, 0)),
        ),
        cost_estimate=cost(0, 2 * bytes_of(*pieces)),
    )(order, *pieces)


def arrivals(group):
    return 0 if group["x_first"] else 1


def add_three(groups, last, total):
    count = len(groups)
    cols = last[0].shape[1]
    axis, size = groups[0]["axis"], groups[0]["size"]
    tile = tile_of(total, 4)
    specs = []
    for g in groups:
        skip = arrivals(g) * (size // tile) if axis == 0 else 0
        side = arrivals(g) if axis == 1 else 0
        specs.append(pl.BlockSpec((tile, cols), lambda i: (i, 0)))
        specs.append(pl.BlockSpec((tile, cols), lambda i, skip=skip, side=side: (i + skip, side)))
        specs.append(pl.BlockSpec((tile, cols), lambda i: (i, 0)))

    def body(*refs):
        for e in range(count):
            held, here, after = (refs[3 * e + k][...].astype(F32) for k in range(3))
            refs[3 * count][e] = held + here + after

    return pl.pallas_call(
        body,
        out_shape=jax.ShapeDtypeStruct((count, total, cols), F32),
        grid=(total // tile,),
        in_specs=specs,
        out_specs=pl.BlockSpec((count, tile, cols), lambda i: (0, i, 0)),
        cost_estimate=cost(3 * count * total * cols, 10 * count * total * cols),
    )(*[v for g, w in zip(groups, last) for v in (g["held"], g["near"], w)])


def add_three_turned(group, last, columns):
    rows, cols = last.shape
    side = arrivals(group)
    spec = pl.BlockSpec((rows, cols), lambda i: (0, 0))

    def body(held_ref, here_ref, last_ref, *out_refs):
        for ref, (start, count) in zip(out_refs, columns):
            part = slice(start, start + count)
            total = held_ref[:, part].astype(F32) + here_ref[:, part].astype(F32)
            ref[...] = (total + last_ref[:, part].astype(F32)).T

    return pl.pallas_call(
        body,
        out_shape=[jax.ShapeDtypeStruct((n, rows), F32) for _, n in columns],
        grid=(1,),
        in_specs=[spec, pl.BlockSpec((rows, cols), lambda i: (side, 0)), spec],
        out_specs=[pl.BlockSpec((n, rows), lambda i: (0, 0)) for _, n in columns],
        cost_estimate=cost(3 * rows * cols, 10 * rows * cols),
    )(group["held"], group["near"], last)


def join_columns(pieces):
    rows, width = pieces[0].shape
    count = len(pieces)
    tile = tile_of(rows, max(2, bytes_of(*pieces) >> 20))

    def body(*refs):
        for i in range(count):
            refs[count][:, i * width : (i + 1) * width] = refs[i][...]

    return pl.pallas_call(
        body,
        out_shape=jax.ShapeDtypeStruct((rows, count * width), pieces[0].dtype),
        grid=(rows // tile,),
        in_specs=[pl.BlockSpec((tile, width), lambda i: (i, 0))] * count,
        out_specs=pl.BlockSpec((tile, count * width), lambda i: (i, 0)),
        cost_estimate=cost(0, 2 * bytes_of(*pieces)),
    )(*pieces)


def join_rows(pieces, count, joined=None):
    experts, rows, cols = pieces[0].shape
    given = len(pieces)
    tile = tile_of(rows, max(2, bytes_of(*pieces) >> 20))
    shape = jax.ShapeDtypeStruct((count, rows, cols), pieces[0].dtype)
    if joined is None:
        places = [i for i in range(count) if given == count or i % 4 != 2]

        def body(*refs):
            for e in range(experts):
                for ref, place in zip(refs, places):
                    refs[given + e][place] = ref[e]

        out = pl.pallas_call(
            body,
            out_shape=[shape] * experts,
            grid=(rows // tile,),
            in_specs=[pl.BlockSpec((experts, tile, cols), lambda i: (0, i, 0))] * given,
            out_specs=[pl.BlockSpec((count, tile, cols), lambda i: (0, i, 0))] * experts,
            cost_estimate=cost(0, 2 * bytes_of(*pieces)),
        )(*pieces)
        return [v.reshape(count * rows, cols) for v in out]
    whole = [v.reshape(given, count // given, rows, cols) for v in joined]

    def fill(*refs):
        for e in range(experts):
            for i in range(given):
                refs[given + experts + e][i, 0] = refs[i][e]

    out = pl.pallas_call(
        fill,
        out_shape=[jax.ShapeDtypeStruct(v.shape, v.dtype) for v in whole],
        grid=(rows // tile,),
        in_specs=[pl.BlockSpec((experts, tile, cols), lambda i: (0, i, 0))] * given
        + [pl.BlockSpec(memory_space=pl.ANY)] * experts,
        out_specs=[pl.BlockSpec((given, 1, tile, cols), lambda i: (0, 2, i, 0))] * experts,
        input_output_aliases={given + e: e for e in range(experts)},
        cost_estimate=cost(0, 2 * bytes_of(*pieces)),
    )(*pieces, *whole)
    return [v.reshape(count * rows, cols) for v in out]


def pick_of(head, heads):
    half = QR // 2
    row = lax.broadcasted_iota(jnp.int32, (QR, heads * QR), 0)
    lane = lax.broadcasted_iota(jnp.int32, (QR, heads * QR), 1)
    place = (row // half) * (heads * half) + head * half + row % half
    return jnp.where(lane == place, 1.0, 0.0).astype(BF16)


def attend(plain, turned, pairs, rope, query_pos, key_pos, seqs, heads):
    span = plain.shape[0] // seqs
    keys = pairs.shape[0] // seqs
    scale = (QN + QR) ** (-0.5)
    rope_cols = heads * QR

    def body(plain_ref, turned_ref, pairs_ref, rope_ref, qpos_ref, kpos_ref, probs_ref, out_ref):
        turned_own = dot_nt(turned_ref[...], pick_of(pl.program_id(1), heads)).astype(BF16)
        logits = dot_nt(plain_ref[...], pairs_ref[:, :QN]) + dot_nt(turned_own, rope_ref[...])
        seen = qpos_ref[...] >= kpos_ref[...]
        exps = jnp.where(seen, jnp.exp(logits * scale), 0.0)
        probs = (exps / jnp.sum(exps, axis=-1, keepdims=True)).astype(BF16)
        probs_ref[0] = probs
        out_ref[...] = dot_nn(probs, pairs_ref[:, QN:]).astype(BF16)

    return pl.pallas_call(
        body,
        out_shape=(
            jax.ShapeDtypeStruct((seqs * heads, span, keys), BF16),
            jax.ShapeDtypeStruct((seqs * span, heads * VD), BF16),
        ),
        grid=(seqs, heads),
        in_specs=[
            pl.BlockSpec((span, QN), lambda s, h: (s, h)),
            pl.BlockSpec((span, rope_cols), lambda s, h: (s, 0)),
            pl.BlockSpec((keys, QN + VD), lambda s, h: (s, h)),
            pl.BlockSpec((keys, QR), lambda s, h: (s, 0)),
            pl.BlockSpec((span, 1), lambda s, h: (0, 0)),
            pl.BlockSpec((1, keys), lambda s, h: (0, 0)),
        ],
        out_specs=(
            pl.BlockSpec((1, span, keys), lambda s, h: (s * heads + h, 0, 0)),
            pl.BlockSpec((span, VD), lambda s, h: (s, h)),
        ),
        cost_estimate=cost(
            2 * seqs * heads * span * keys * (QN + rope_cols + VD),
            bytes_of(plain, turned, pairs) + 2 * seqs * heads * span * keys,
            seqs * heads * span * keys,
        ),
    )(plain, turned, pairs, rope, query_pos[:, None], key_pos[None, :])


def attend_back(plain, turned, pairs, rope, probs, grad_heads, seqs, heads):
    span = plain.shape[0] // seqs
    keys = pairs.shape[0] // seqs
    scale = (QN + QR) ** (-0.5)
    rope_cols = heads * QR

    def body(
        plain_ref, turned_ref, pairs_ref, rope_ref, probs_ref, grad_ref,
        dplain_ref, dturned_ref, dpairs_ref, drope_ref,
    ):
        head = pl.program_id(1)
        pick = pick_of(head, heads)
        turned_own = dot_nt(turned_ref[...], pick).astype(BF16)
        probs_low = probs_ref[0]
        probs_f = probs_low.astype(F32)
        grad = grad_ref[...]
        grad_probs = dot_nt(grad, pairs_ref[:, QN:])
        delta = jnp.sum(probs_f * grad_probs, axis=-1, keepdims=True)
        grad_logits = (probs_f * (grad_probs - delta) * scale).astype(BF16)
        dplain_ref[...] = dot_nn(grad_logits, pairs_ref[:, :QN]).astype(BF16)
        dpairs_ref[:, QN:] = dot_tn(probs_low, grad).astype(BF16)
        dpairs_ref[:, :QN] = dot_tn(grad_logits, plain_ref[...]).astype(BF16)
        turned_part = dot_nn(dot_nn(grad_logits, rope_ref[...]).astype(BF16), pick)
        rope_part = dot_tn(grad_logits, turned_own)

        @pl.when(head == 0)
        def _():
            dturned_ref[...] = turned_part
            drope_ref[...] = rope_part

        @pl.when(head > 0)
        def _():
            dturned_ref[...] += turned_part
            drope_ref[...] += rope_part

    return pl.pallas_call(
        body,
        out_shape=(
            jax.ShapeDtypeStruct(plain.shape, BF16),
            jax.ShapeDtypeStruct(turned.shape, F32),
            jax.ShapeDtypeStruct(pairs.shape, BF16),
            jax.ShapeDtypeStruct(rope.shape, F32),
        ),
        grid=(seqs, heads),
        in_specs=[
            pl.BlockSpec((span, QN), lambda s, h: (s, h)),
            pl.BlockSpec((span, rope_cols), lambda s, h: (s, 0)),
            pl.BlockSpec((keys, QN + VD), lambda s, h: (s, h)),
            pl.BlockSpec((keys, QR), lambda s, h: (s, 0)),
            pl.BlockSpec((1, span, keys), lambda s, h: (s * heads + h, 0, 0)),
            pl.BlockSpec((span, VD), lambda s, h: (s, h)),
        ],
        out_specs=(
            pl.BlockSpec((span, QN), lambda s, h: (s, h)),
            pl.BlockSpec((span, rope_cols), lambda s, h: (s, 0)),
            pl.BlockSpec((keys, QN + VD), lambda s, h: (s, h)),
            pl.BlockSpec((keys, QR), lambda s, h: (s, 0)),
        ),
        cost_estimate=cost(
            2 * seqs * heads * span * keys * (2 * QN + 2 * VD + 2 * QR),
            2 * bytes_of(plain, turned, pairs) + bytes_of(probs),
        ),
    )(plain, turned, pairs, rope, probs, grad_heads)


def pad_cols(values, width):
    return jnp.pad(values, ((0, 0), (0, width - values.shape[1])))


def up_to(count, step):
    return -(-count // step) * step


class Plan:
    def __init__(self, sizes):
        self.dp = sizes["dp"]
        self.ctx = sizes["ctx"]
        self.fast = self.dp == 4 and self.ctx == 2
        if self.fast:
            me = lax.axis_index("dp") * 2 + lax.axis_index("ctx")
            ids = jnp.arange(8, dtype=jnp.int32)
            y, core, x = (ids >> 1) & 1, ids >> 2, (ids ^ (ids >> 1)) & 1
            self.order = ((4 * y + 2 * core + x) ^ me).astype(jnp.int32)
            apart = ids ^ me
            y, core, x = apart >> 2, (apart >> 1) & 1, apart & 1
            self.inverse = (4 * core + x + y * (3 - 2 * x)).astype(jnp.int32)

    @staticmethod
    def over_core(values):
        return lax.ppermute(values, "dp", [(i, i ^ 1) for i in range(4)])

    @staticmethod
    def over_y(values):
        return lax.ppermute(values, "dp", [(i, i ^ 2) for i in range(4)])

    @staticmethod
    def over_x(values):
        return lax.ppermute(values, "ctx", [(0, 1), (1, 0)])

    def tie(self, values, *after):
        return lax.optimization_barrier((values, after))[0] if self.fast else values

    def to_own(self, values):
        return column_blocks(self.order, values) if self.fast else values

    def to_natural(self, values):
        return column_blocks(self.inverse, values) if self.fast else values

    def spread(self, shard):
        if not self.fast:
            return ()
        return (self.over_x(shard), self.over_y(shard))

    def collect(self, name, shard, near, axis, x_last, *after):
        if not self.fast:
            full = lax.all_gather(shard, ("dp", "ctx"), axis=axis, tiled=True)
            return (list(full), lambda *after: list(full)) if shard.ndim == 3 else full
        from_x, from_y = near
        from_xy = self.over_x(from_y) if x_last else self.over_y(from_x)
        own = [shard, from_x, from_xy, from_y]
        if shard.ndim == 3:
            early = self.tie([shard, from_x, from_y], *after)
            early = early + [self.over_core(v) for v in early]
            joined = join_rows(early, 8)

            def rest(*after):
                late = self.tie(from_xy, joined, *after)
                late = [late, self.over_core(late)]
                return join_rows(late, 8, joined)

            return joined, rest
        own[2] = self.tie(from_xy, *after)
        pieces = own + [self.over_core(v) for v in own]
        if name == EXPAND:
            return place_rows(self.order, pieces)
        if axis == 0:
            return join_rows([v[None] for v in pieces], 8)[0]
        return join_columns(pieces)

    def over(self, values, first, x_first):
        return self.over_x(values) if first == x_first else self.over_y(values)

    def begin(self, name, left_in, right_in, size, axis, x_first):
        if not self.fast:
            return self.begin_given(name, dot_tn(left_in, right_in).astype(BF16), size, axis, x_first)
        half = 4 * size

        def part(a, b):
            if axis == 0:
                return dot_tn(left_in[:, a:b], right_in)
            return dot_tn(left_in, right_in[:, a:b])

        sent = self.over_core(part(half, 2 * half).astype(BF16))
        held = (part(0, half) + sent.astype(F32)).astype(BF16)
        return {"held": held, "x_first": x_first, "name": name, "size": size, "axis": axis}

    def cut(self, group, name, i, count=1):
        size = group["size"]
        return lax.slice_in_dim(group[name], i * size, (i + count) * size, axis=group["axis"])

    def begin_given(self, name, whole, size, axis, x_first):
        if not self.fast:
            held = lax.psum_scatter(whole, ("dp", "ctx"), scatter_dimension=axis, tiled=True)
        else:
            sent = self.over_core(lax.slice_in_dim(whole, 4 * size, 8 * size, axis=axis))
            held = lax.slice_in_dim(whole, 0, 4 * size, axis=axis).astype(F32)
            held = (held + sent.astype(F32)).astype(BF16)
        return {"held": held, "x_first": x_first, "name": name, "size": size, "axis": axis}

    def first(self, groups):
        if not self.fast:
            return
        for g in groups:
            both = self.cut(g, "held", 1 if g["x_first"] else 2, 2)
            g["near"] = self.over(both, True, g["x_first"])

    def second(self, groups, *after):
        if not self.fast:
            return
        near = self.tie([g["near"] for g in groups], *after)
        for g, v in zip(groups, near):
            g["near"] = v
            kept = self.cut(g, "held", 3 if g["x_first"] else 1).astype(F32)
            there = self.cut(g, "near", 1 if g["x_first"] else 0).astype(F32)
            g["last"] = self.over((kept + there).astype(BF16), False, g["x_first"])

    def finish(self, groups, rows, *after):
        if not self.fast:
            return jnp.stack([g["held"][:rows].astype(F32) for g in groups])
        last = self.tie([g["last"] for g in groups], *after)
        return add_three(groups, last, rows)

    def finish_turned(self, group, columns, *after):
        if not self.fast:
            return [group["held"][:, a : a + n].astype(F32) for a, n in columns]
        last = self.tie(group["last"], *after)
        return [v.T for v in add_three_turned(group, last, columns)]


def scatter_mp(values, n_mp, direct, tie):
    if not direct:
        return lax.psum_scatter(values, "mp", scatter_dimension=0, tiled=True).astype(F32)
    share = values.shape[0] // n_mp
    me = lax.axis_index("mp")

    def part(i):
        return lax.dynamic_slice_in_dim(values, (i % n_mp) * share, share, axis=0)

    arrived = []
    for step in range(1, n_mp):
        path = [(i, (i + step) % n_mp) for i in range(n_mp)]
        arrived.append(lax.ppermute(part(me + step), "mp", path))
    return sum((v.astype(F32) for v in tie(arrived)), part(me).astype(F32))


def gather_mp(values, n_mp, direct, tie):
    if not direct:
        return lax.all_gather(values, "mp", axis=0, tiled=True)
    share = values.shape[0]
    me = lax.axis_index("mp")
    others = [values]
    for step in range(1, n_mp):
        path = [(i, (i + step) % n_mp) for i in range(n_mp)]
        others.append(lax.ppermute(values, "mp", path))
    whole = jnp.zeros((n_mp * share,) + values.shape[1:], values.dtype)
    for step, other in enumerate(tie(others)):
        whole = lax.dynamic_update_slice_in_dim(
            whole, other, ((me - step) % n_mp) * share, axis=0
        )
    return whole


def sum_mp(values, n_mp):
    total = values
    for step in range(1, n_mp):
        path = [(i, (i + step) % n_mp) for i in range(n_mp)]
        total = total + lax.ppermute(values, "mp", path)
    return total


def local(
    sizes,
    block_input,
    norm_one_gain,
    query_weight,
    latent_weight,
    latent_gain,
    expand_weight,
    output_weight,
    norm_two_gain,
    router_weight,
    expert_gate,
    expert_up,
    expert_down,
    shared_gate,
    shared_up,
    shared_down,
    routes,
    route_slots,
    cotangent,
):
    plan = Plan(sizes)
    fast = plan.fast
    n_mp = sizes["mp"]
    mp_index = lax.axis_index("mp")
    seq_count, span_len = block_input.shape[0], block_input.shape[1]
    rows = seq_count * span_len
    shard_rows = rows // n_mp
    head_dim = QN + QR
    q_cols = query_weight.shape[1]
    local_heads = q_cols // head_dim
    experts_here = expert_gate.shape[0]
    experts_all = router_weight.shape[1]
    hidden = expert_gate.shape[2]
    shared_cols = shared_gate.shape[1]
    shared_pad = up_to(shared_cols, 2 * LANES)
    block = norm_one_gain.shape[0]
    rank_block = expand_weight.shape[0]

    half_dim = QR // 2
    both_halves = local_heads * half_dim

    if fast:
        gains = jnp.concatenate([norm_one_gain, norm_two_gain, latent_gain]).astype(F32)[None]
        gains_x = plan.over_x(gains)
        gains = jnp.concatenate([gains, gains_x], axis=0)
        gains_y = plan.over_y(gains)
        gains = jnp.concatenate([gains, gains_y[1:], gains_y[:1]], axis=0)
        gains_core = plan.over_core(gains)
        gains = jnp.concatenate([gains, gains_core], axis=0)
        gain_one = gains[:, :block].reshape(8 * block)
        gain_two = gains[:, block : 2 * block].reshape(8 * block)
        rank_rel = gains[:, 2 * block :]
        place = (plan.inverse[:, None] == jnp.arange(8, dtype=jnp.int32)[None, :]).astype(F32)
        gain_latent = jnp.sum(place[:, :, None] * rank_rel[None, :, :], axis=1).reshape(KVR)
    latent_cols = KVR + QR
    latent_shard = jnp.concatenate([latent_weight, router_weight], axis=1)
    latent_near = plan.spread(latent_shard)
    expand_near = plan.spread(expand_weight)
    output_near = plan.spread(output_weight)
    query_weight = plan.tie(query_weight, *latent_near)
    by_head = query_weight.reshape(block, local_heads, head_dim)
    query_shard = jnp.concatenate(
        [
            by_head[:, :, :QN].reshape(block, local_heads * QN),
            by_head[:, :, QN : QN + half_dim].reshape(block, both_halves),
            by_head[:, :, QN + half_dim :].reshape(block, both_halves),
        ],
        axis=1,
    )
    query_near = plan.spread(query_shard)
    latent_router = plan.collect(LAT, latent_shard, latent_near, 0, True)
    latent_full = latent_router[:, :latent_cols]
    router_full = latent_router[:, latent_cols:]
    if not fast:
        gain_one = lax.all_gather(norm_one_gain, ("dp", "ctx"), tiled=True).astype(F32)
        gain_two = lax.all_gather(norm_two_gain, ("dp", "ctx"), tiled=True).astype(F32)
        gain_latent = lax.all_gather(latent_gain, ("dp", "ctx"), tiled=True).astype(F32)

    ctx_index = lax.axis_index("ctx")
    frequencies = 10000.0 ** (-jnp.arange(half_dim, dtype=F32) / half_dim)
    steps = jnp.arange(span_len, dtype=jnp.int32)
    query_pos = ctx_index * span_len + steps
    angles = jnp.tile(query_pos.astype(F32)[:, None] * frequencies[None, :], (seq_count, 1))
    cosines = jnp.cos(angles)
    sines = jnp.sin(angles)
    lanes = jnp.arange(both_halves, dtype=jnp.int32) % half_dim
    all_frequencies = 10000.0 ** (-lanes.astype(F32) / half_dim)
    all_angles = jnp.tile(query_pos.astype(F32), seq_count)[:, None] * all_frequencies[None, :]
    cos_heads = jnp.cos(all_angles)
    sin_heads = jnp.sin(all_angles)

    row_start = mp_index * shard_rows

    def own_rows(values):
        return lax.dynamic_slice_in_dim(values, row_start, shard_rows, axis=0)

    x_low = plan.to_own(block_input.reshape(rows, D))
    x_own = own_rows(x_low).astype(F32)
    h_one = norm_rows(x_low.astype(F32), gain_one)[0].astype(BF16)
    latent = dot_nn(h_one, latent_router)[:, :latent_cols]
    comp_f = norm_rows(latent[:, :KVR], gain_latent)[0]
    key_rope = rotate(latent[:, KVR:], cosines, sines)
    shared_kv = jnp.concatenate([comp_f, key_rope], axis=1).astype(BF16)

    shared_kv = shared_kv.reshape(seq_count, span_len, KVR + QR)
    if plan.ctx == 2:
        other_kv = plan.over_x(shared_kv)
        kv_all = jnp.concatenate([shared_kv, other_kv], axis=1)
        key_pos = jnp.concatenate([query_pos, (1 - ctx_index) * span_len + steps])
    else:
        kv_all = lax.all_gather(shared_kv, "ctx", axis=1, tiled=True)
        key_pos = jnp.arange(plan.ctx * span_len, dtype=jnp.int32)
    down_shards = [expert_down[e] for e in range(experts_here)]
    down_shards = plan.tie(down_shards, shared_kv)
    down_near = [plan.spread(v) for v in down_shards]
    gate_shard = plan.tie(expert_gate, shared_kv)
    gate_near = plan.spread(gate_shard)

    query_near, expand_near, output_near = (
        plan.tie(v, shared_kv) for v in (query_near, expand_near, output_near)
    )
    query_full = plan.collect(QUERY, query_shard, query_near, 0, False)
    expand_full = plan.collect(EXPAND, expand_weight, expand_near, 0, False)
    output_full = plan.collect(OUTPUT, output_weight, output_near, 1, True)
    seq_len = key_pos.shape[0]
    comp_all = kv_all[..., :KVR].reshape(seq_count * seq_len, KVR)
    rope_all = kv_all[..., KVR:].reshape(seq_count * seq_len, QR)
    q_raw = dot_nn(h_one, query_full)
    plain_cols = local_heads * QN
    plain = q_raw[:, :plain_cols].astype(BF16)
    first = q_raw[:, plain_cols : plain_cols + both_halves]
    second = q_raw[:, plain_cols + both_halves :]
    turned = jnp.concatenate(
        [first * cos_heads - second * sin_heads, second * cos_heads + first * sin_heads], axis=1
    ).astype(BF16)
    pairs = dot_nn(comp_all, expand_full).astype(BF16)
    probs, heads_flat = attend(
        plain, turned, pairs, rope_all, query_pos, key_pos, seq_count, local_heads
    )
    attn_part = dot_nn(heads_flat, output_full).astype(BF16)
    attn_sum = lax.psum_scatter(attn_part, "mp", scatter_dimension=0, tiled=True)

    cotangent, route_rows, slot_rows = plan.tie(
        (cotangent, routes.reshape(rows, TOP), route_slots.reshape(rows, TOP)), attn_part
    )
    g_low = plan.to_own(cotangent.reshape(rows, D))
    g_own = own_rows(g_low).astype(F32)
    slot_ids = jnp.arange(rows, dtype=jnp.int32)
    hits = []
    for e in range(experts_here):
        named = route_rows == mp_index * experts_here + e
        slot = jnp.sum(jnp.where(named, slot_rows + 1, 0), axis=-1) - 1
        hits.append(slot[:, None] == slot_ids[None, :])
    one_hot = [v.astype(BF16) for v in hits]
    both_hot = jnp.concatenate(one_hot, axis=1)
    g_slots = [dot_tn(v, g_low).astype(BF16) for v in one_hot]
    down_near = [plan.tie(v, attn_part) for v in down_near]
    attn_sum = plan.tie(attn_sum, *g_slots)
    up_shard = plan.tie(expert_up, attn_part)
    up_near = plan.spread(up_shard)
    shared_gate, shared_up, shared_down = plan.tie((shared_gate, shared_up, shared_down), *g_slots)
    shared_shard = jnp.concatenate(
        [pad_cols(shared_gate, shared_pad), pad_cols(shared_up, shared_pad)], axis=1
    )
    sdown_shard = jnp.pad(shared_down, ((0, shared_pad - shared_cols), (0, 0)))
    shared_near = plan.spread(shared_shard)
    sdown_near = plan.spread(sdown_shard)

    mixed = x_own + attn_sum.astype(F32)
    h_two_f, normed_two, inverse_two = norm_rows(mixed, gain_two)
    h_two_own = h_two_f.astype(BF16)
    h_two = lax.all_gather(h_two_own, "mp", axis=0, tiled=True)

    gate_near = plan.tie(gate_near, h_two_own)
    gate_joined, gate_rest = plan.collect(GATE, gate_shard, gate_near, 1, True)
    up_near = plan.tie(up_near, gate_joined)
    up_joined, up_rest = plan.collect(UP, up_shard, up_near, 1, False)
    after, down_full, act_back = up_joined, [], []
    for e in range(experts_here):
        full = plan.collect(DOWN, down_shards[e], down_near[e], 1, e % 2 == 0, after)
        down_full.append(full)
        act_back.append(dot_nt(g_slots[e], full).astype(BF16))
        after = act_back[e]
    gate_full = gate_rest(after)

    dispatched = [dot_tn(v, h_two).astype(BF16) for v in one_hot]
    gate_all = plan.tie([dot_nn(dispatched[e], gate_full[e]) for e in range(experts_here)])
    up_full = up_rest(gate_all)
    router_exp = jnp.exp(dot_nn(h_two, router_full))
    router_probs = router_exp / jnp.sum(router_exp, axis=-1, keepdims=True)
    probs_here = lax.dynamic_slice_in_dim(router_probs, mp_index * experts_here, experts_here, 1)
    slot_gate = [
        jnp.sum(jnp.where(hits[e], probs_here[:, e : e + 1], 0.0), axis=0)
        for e in range(experts_here)
    ]
    grad_gates, grad_ups, act_gated, slot_grads = [], [], [], []
    for e in range(experts_here):
        gate_vals = gate_all[e]
        up_vals = dot_nn(dispatched[e], up_full[e])
        sig = jax.nn.sigmoid(gate_vals)
        act = gate_vals * sig * up_vals
        gated = slot_gate[e][:, None]
        back = act_back[e].astype(F32)
        slot_grads.append(jnp.sum(back * act, axis=-1))
        back = back * gated
        grad_gate = (back * up_vals * sig * (1.0 + gate_vals * (1.0 - sig))).astype(BF16)
        grad_up = (back * gate_vals * sig).astype(BF16)
        grad_gate, grad_up, act = plan.tie((grad_gate, grad_up, (act * gated).astype(BF16)))
        grad_gates.append(grad_gate)
        grad_ups.append(grad_up)
        act_gated.append(act)


    shared_near, sdown_near = plan.tie((shared_near, sdown_near), h_two_own)
    shared_full = plan.collect(SHARED, shared_shard, shared_near, 0, False, act_gated)
    sdown_full = plan.collect(SDOWN, sdown_shard, sdown_near, 1, True, shared_full)
    shared_back = dot_nt(g_low, sdown_full)
    shared_vals = dot_nn(h_two, shared_full)
    shared_a = shared_vals[:, :shared_pad]
    shared_b = shared_vals[:, shared_pad:]
    shared_sig = jax.nn.sigmoid(shared_a)
    shared_act = (shared_a * shared_sig * shared_b).astype(BF16)
    grad_shared_gate = shared_back * shared_b * shared_sig * (1.0 + shared_a * (1.0 - shared_sig))
    grad_shared_up = shared_back * shared_a * shared_sig
    grad_shared = jnp.concatenate([grad_shared_gate, grad_shared_up], axis=1).astype(BF16)

    grad_slots = []
    for e in range(experts_here):
        grad_slot = dot_nt(grad_gates[e], gate_full[e]) + dot_nt(grad_ups[e], up_full[e])
        grad_slots.append(grad_slot.astype(BF16))
    grad_h_two = dot_nn(both_hot, jnp.concatenate(grad_slots, axis=0)) + dot_nt(
        grad_shared, shared_full
    )
    expert_ids = jnp.arange(LANES, dtype=jnp.int32)
    grad_probs_part = jnp.zeros((rows, LANES), F32)
    for e in range(experts_here):
        of_token = jnp.sum(jnp.where(hits[e], slot_grads[e][None, :], 0.0), axis=1)
        grad_probs_part = grad_probs_part + jnp.where(
            expert_ids[None, :] == mp_index * experts_here + e, of_token[:, None], 0.0
        )
    back_part = jnp.concatenate([grad_h_two.astype(BF16), grad_probs_part.astype(BF16)], axis=1)
    back_sum = lax.psum_scatter(back_part, "mp", scatter_dimension=0, tiled=True).astype(F32)

    acts, slots_g, acts_s, g_late, h_late, shared_late = plan.tie(
        (act_gated, g_slots, shared_act, g_low, h_two, grad_shared), back_part
    )
    sums_one = [
        plan.begin(ONE, h_late, shared_late, block, 0, False),
        plan.begin(ONE, acts_s, g_late, block, 1, True),
    ] + [
        plan.begin(ONE, acts[e], slots_g[e], block, 1, e % 2 == 0)
        for e in range(experts_here)
    ]
    plan.first(sums_one)
    back_sum = plan.tie(back_sum, *[g["held"] for g in sums_one])

    probs_own = own_rows(router_probs)
    grad_probs = back_sum[:, D : D + experts_all]
    grad_logits = (
        probs_own * (grad_probs - jnp.sum(probs_own * grad_probs, axis=-1, keepdims=True))
    ).astype(BF16)
    grad_two = back_sum[:, :D] + dot_nt(grad_logits, router_full)
    grad_norm, norm_two_part = norm_back(grad_two, normed_two, inverse_two, gain_two)
    grad_mixed = g_own + grad_norm
    mixed_part = jnp.concatenate([grad_mixed.astype(BF16), pad_cols(grad_logits, LANES)], axis=1)
    mixed_all = lax.all_gather(mixed_part, "mp", axis=0, tiled=True)

    acts_out, shared_act_out = plan.tie((act_gated, shared_act), mixed_part)
    expert_out = [dot_nn(acts_out[e], down_full[e]).astype(BF16) for e in range(experts_here)]
    ff_part = dot_nn(both_hot, jnp.concatenate(expert_out, axis=0)) + dot_nn(
        shared_act_out, sdown_full
    )
    ff_part = ff_part.astype(BF16)
    ff_sum = lax.psum_scatter(ff_part, "mp", scatter_dimension=0, tiled=True).astype(F32)


    sent_rows, gates_late = plan.tie((dispatched, grad_gates), mixed_part)
    sums_two = [
        plan.begin(TWO, sent_rows[e], gates_late[e], block, 0, e % 2 == 0)
        for e in range(experts_here)
    ]
    plan.first(sums_two)
    mixed_all = plan.tie(mixed_all, *[g["held"] for g in sums_two])

    grad_low = mixed_all[:, :D]
    grad_heads = dot_nt(grad_low, output_full).astype(BF16)
    dplain, dturned, grad_pairs, grad_rope = attend_back(
        plain, turned, pairs, rope_all, probs, grad_heads, seq_count, local_heads
    )
    back_first = dturned[:, :both_halves]
    back_second = dturned[:, both_halves:]
    grad_q_raw = jnp.concatenate(
        [
            dplain,
            (back_first * cos_heads + back_second * sin_heads).astype(BF16),
            (back_second * cos_heads - back_first * sin_heads).astype(BF16),
        ],
        axis=1,
    )
    query_part = dot_nt(grad_q_raw, query_full).astype(BF16)
    grad_one = lax.psum_scatter(query_part, "mp", scatter_dimension=0, tiled=True).astype(F32)
    grad_comp = dot_nt(grad_pairs, expand_full).reshape(seq_count, seq_len, KVR)
    grad_rope = grad_rope.reshape(seq_count, seq_len, QR)
    grad_kv = jnp.concatenate([grad_comp, grad_rope], axis=-1)
    if plan.ctx == 2:
        to_other = grad_kv[:, span_len:].astype(BF16)
        from_other = plan.over_x(to_other)
        grad_kv = grad_kv[:, :span_len] + from_other.astype(F32)
    else:
        to_other = ()
        grad_kv = grad_kv.reshape(seq_count, plan.ctx, span_len, KVR + QR).transpose(1, 0, 2, 3)
        grad_kv = grad_kv.reshape(plan.ctx * rows, KVR + QR).astype(BF16)
        grad_kv = lax.psum_scatter(grad_kv, "ctx", scatter_dimension=0, tiled=True)
    sent_late, ups_late = plan.tie((dispatched, grad_ups), query_part, to_other)
    plan.second(sums_one, query_part, to_other)
    plan.second(sums_two, query_part, to_other)
    sums_three = [
        plan.begin(THREE, sent_late[e], ups_late[e], block, 0, e % 2 == 1)
        for e in range(experts_here)
    ]
    plan.first(sums_three)
    grad_kv = scatter_mp(
        grad_kv.reshape(rows, KVR + QR).astype(BF16),
        n_mp,
        fast,
        lambda values: plan.tie(values, *[g["held"] for g in sums_three]),
    )
    _, comp_normed, comp_inverse = norm_rows(own_rows(latent)[:, :KVR], gain_latent)
    grad_comp_in, latent_gain_part = norm_back(
        grad_kv[:, :KVR], comp_normed, comp_inverse, gain_latent
    )
    grad_latent = jnp.concatenate(
        [grad_comp_in, rotate(grad_kv[:, KVR:], own_rows(cosines), -own_rows(sines))], axis=1
    ).astype(BF16)
    grad_one = grad_one + dot_nt(grad_latent, latent_full)
    _, normed_one, inverse_one = norm_rows(x_own, gain_one)
    grad_tokens, norm_one_part = norm_back(grad_one, normed_one, inverse_one, gain_one)
    input_own = plan.to_natural((grad_mixed + grad_tokens).astype(BF16))
    input_grad = lax.all_gather(input_own, "mp", axis=0, tiled=True)

    result_own = plan.to_natural((mixed + ff_sum).astype(BF16))
    result_own = plan.tie(result_own, mixed_all)
    result = lax.all_gather(result_own, "mp", axis=0, tiled=True)

    h_tail, heads_tail, low_tail, q_tail, comp_tail, pairs_tail = plan.tie(
        (h_one, heads_flat, grad_low, grad_q_raw, comp_all, grad_pairs),
        [g["held"] for g in sums_three],
    )
    sums_four = [
        plan.begin(FOUR, heads_tail, low_tail, block, 1, True),
        plan.begin(FOUR, h_tail, q_tail, block, 0, False),
    ]
    expand_whole = dot_tn(comp_tail, pairs_tail).astype(BF16)
    if fast:
        expand_whole = row_blocks(plan.order, expand_whole)
    sums_four.append(plan.begin_given(FOUR, expand_whole, rank_block, 0, True))
    plan.first(sums_four)
    held_four = [g["held"] for g in sums_four]
    plan.second(sums_three)
    sgate_grad, sup_grad = plan.finish_turned(
        sums_one[0], [(0, shared_cols), (shared_pad, shared_cols)], held_four
    )
    sdown_grad = plan.finish(sums_one[1:2], shared_cols, held_four)[0]
    down_grads = plan.finish(sums_one[2:], hidden, held_four)
    gate_grads = plan.finish(sums_two, block, held_four)
    latent_all = gather_mp(grad_latent, n_mp, fast, lambda values: plan.tie(values, held_four))
    plan.second(sums_four)
    sums_five = [plan.begin(FIVE, h_tail, latent_all, block, 0, False)]
    plan.first(sums_five)
    plan.second(sums_five)
    up_grads = plan.finish(sums_three, block, latent_all)
    output_grad, query_grad, expand_grad = (
        plan.finish([g], n, latent_all)[0]
        for g, n in zip(sums_four, (output_weight.shape[0], block, rank_block))
    )
    (latent_grad,) = plan.finish_turned(sums_five[0], [(0, latent_cols)])
    query_grad = jnp.concatenate(
        [
            query_grad[:, :plain_cols].reshape(block, local_heads, QN),
            query_grad[:, plain_cols:][:, :both_halves].reshape(block, local_heads, half_dim),
            query_grad[:, plain_cols + both_halves :].reshape(block, local_heads, half_dim),
        ],
        axis=2,
    ).reshape(block, q_cols)

    router_part = dot_tn(mixed_all[:, D : D + experts_all], h_two)
    if fast:
        to_rel = (plan.order[:, None] == jnp.arange(8, dtype=jnp.int32)[None, :]).astype(F32)
        latent_rel = jnp.sum(
            to_rel[:, :, None] * latent_gain_part.reshape(1, 8, rank_block), axis=1
        )
        router_once = jnp.where(mp_index == 0, router_part, 0.0)
        router_rel = router_once.reshape(experts_all, 8, block).transpose(1, 0, 2)
        small = jnp.concatenate(
            [
                norm_one_part.reshape(8, block),
                norm_two_part.reshape(8, block),
                router_rel.reshape(8, experts_all * block),
                pad_cols(latent_rel, LANES),
            ],
            axis=1,
        )
        small = small[:4] + plan.over_core(small[4:])
        from_y = plan.over_y(small[2:])
        small = small[:2] + jnp.concatenate([from_y[1:], from_y[:1]], axis=0)
        small = small[:1] + plan.over_x(small[1:])
        small = sum_mp(small, n_mp)[0]
        norm_one_grad = small[:block]
        norm_two_grad = small[block : 2 * block]
        router_grad = small[2 * block : (2 + experts_all) * block].reshape(experts_all, block).T
        latent_gain_grad = small[(2 + experts_all) * block :][:rank_block]
    else:

        def scatter(values):
            return lax.psum_scatter(values, ("dp", "ctx"), scatter_dimension=0, tiled=True)

        norm_one_grad = scatter(lax.psum(norm_one_part, "mp"))
        norm_two_grad = scatter(lax.psum(norm_two_part, "mp"))
        latent_gain_grad = scatter(lax.psum(latent_gain_part, "mp"))
        router_grad = scatter(router_part.T)

    return (
        result.reshape(seq_count, span_len, D),
        input_grad.reshape(seq_count, span_len, D),
        norm_one_grad,
        query_grad,
        latent_grad,
        latent_gain_grad,
        expand_grad,
        output_grad,
        norm_two_grad,
        router_grad,
        gate_grads,
        up_grads,
        down_grads,
        sgate_grad,
        sup_grad,
        sdown_grad,
    )


def solution(mesh):
    both = ("dp", "ctx")
    tokens = P("dp", "ctx", None)
    in_specs = (
        tokens,
        P(both),
        P(both, "mp"),
        P(both, None),
        P(both),
        P(both, "mp"),
        P("mp", both),
        P(both),
        P(both, None),
        P("mp", both, None),
        P("mp", both, None),
        P("mp", None, both),
        P(both, "mp"),
        P(both, "mp"),
        P("mp", both),
        tokens,
        tokens,
        tokens,
    )
    out_specs = (tokens,) + in_specs[:1] + in_specs[1:15]
    sizes = dict(mesh.shape)

    def per_device(*args):
        return local(sizes, *args)

    return jax.shard_map(
        per_device, mesh=mesh, in_specs=in_specs, out_specs=out_specs, check_vma=False
    )
```
